32 devices in a mesh: seq: 16 (over z, y, core), head: 2 (over x).
Axes of the slice: x: 2, y: 2, z: 4, core: 2. Of those that a mesh axis runs over, the one named last changes fastest.
Arguments:
- q_nope: bfloat16 [4096, 8192], P('seq', 'head'), may hold values from -6 to 6
- q_rope: bfloat16 [4096, 4096], P('seq', 'head'), may hold values from -8 to 8
- latent: bfloat16 [4096, 576], P('seq'), may hold values from -8 to 8
- doc_ids: int32 [4096], P('seq'), may hold values from 0 to 15, never falling along the last dimension, each value on 1 to 1280 neighbouring positions
- w_uk: bfloat16 [512, 8192], P(None, 'head'), may hold values from -0.25 to 0.25
- w_uv: bfloat16 [512, 8192], P(None, 'head'), may hold values from -0.25 to 0.25
- w_out: bfloat16 [8192, 3584], P('head', 'seq'), may hold values from -0.375 to 0.375
Outputs:
- projected: bfloat16 [4096, 3584], P('seq', 'head')
The draws below stay inside these ranges and needn't reach their ends.
Inputs may be any that keep to these rules, and one draw needn't show every extreme that they name: `doc_ids`: document ids never fall along the sequence; every document holds 1 to 1280 tokens, and one holds exactly that many.
All inputs are finite; a program needn't handle non-finite values.
Results may differ from the reference program's by a relative error of at most 0.0065.
Values may be sent and summed in bfloat16 or wider, within the bound.
A program may use at most 128 MiB of HBM per device.

```python
import math
import jax
import jax.numpy as jnp
import numpy as np
from jax import lax

HD = 128
ROPE = 64
VD = 128
LAT = 512
HEADS = 64
DOUT = 3584
HOPS = 4
TOK_DEV = 256
TOKENS = 4096
N_SEQ = 16


def rope_parts(key):
    base_key = jax.random.fold_in(key, 101)
    key_one, key_two = jax.random.split(base_key, 2)
    key_rows = jnp.clip(jax.random.normal(key_one, (TOKENS, ROPE), jnp.float32), -8.0, 8.0)
    queries = jnp.clip(jax.random.normal(key_two, (TOKENS, HEADS, ROPE), jnp.float32), -8.0, 8.0)
    return (key_rows, queries.reshape(TOKENS, HEADS * ROPE))


def draw_latent(key, part):
    key_rows, unused_queries = rope_parts(key)
    content_key = jax.random.fold_in(key, 202)
    content = jnp.clip(jax.random.normal(content_key, (TOKENS, LAT), jnp.float32), -8.0, 8.0)
    return jnp.concatenate([content, key_rows], axis=1).astype(jnp.bfloat16)


def draw_q_rope(key, part):
    return rope_parts(key)[1].astype(jnp.bfloat16)


def steps_of(own_key, extent, cuts, smallest, high):
    level, own = 1.0, jax.random.fold_in(own_key, 6)
    for axis_at, shards_of in cuts:
        draws = jnp.exp(jax.random.uniform(jax.random.fold_in(own, axis_at), (shards_of,), jnp.float32, smallest / len(cuts), high / len(cuts)))
        level = level * jnp.repeat(draws, extent[axis_at] // shards_of).reshape([-1 if axis == axis_at else 1 for axis in range(len(extent))])
    return level


def split_up(count, total, bound, slope):
    weights = [(1 << 20) // math.isqrt(standing ** slope) + 1 for standing in range(2, count + 1)]
    spare, given = total - bound - (count - 1), [1] * (count - 1)
    while spare > 0:
        movable = [i for i in range(count - 1) if given[i] < bound]
        pool, remaining = sum([weights[i] for i in movable]), spare
        for i in movable:
            extra = min(bound - given[i], max(1, remaining * weights[i] // pool), spare)
            given[i] = given[i] + extra
            spare = spare - extra
    return np.array([bound] + given)


def uneven(own_key, count, total, bound, lean):
    if count == 2:
        one = jax.random.randint(own_key, (), max(1, total - bound), min(bound, total - 1) + 1)
        return jnp.stack([one, total - one])
    sizes = jnp.asarray(split_up(count, total, bound, lean), jnp.int32)
    twos = (count - 1) // 2
    giver, sink = sizes[1:1 + 2 * twos:2], sizes[2:2 + 2 * twos:2]
    room = jnp.minimum(giver - 1, bound - sink)
    passed = jax.random.randint(jax.random.fold_in(own_key, 1), (twos,), 0, 1 << 20) % (room + 1)
    sizes = sizes.at[1:1 + 2 * twos:2].set(giver - passed).at[2:2 + 2 * twos:2].set(sink + passed)
    return sizes[jax.random.permutation(jax.random.fold_in(own_key, 2), count)]


def gaussian(own_key, shape, spread, bound, cuts=(), kind=jnp.bfloat16):
    entries = jax.random.normal(own_key, shape, jnp.float32) * spread
    if len(cuts) > 0:
        entries = steps_of(own_key, shape, cuts, -0.22, 0.18) * entries
    return jnp.clip(entries, min=-bound, max=bound).astype(kind)


def setup_inputs(seed: int = 0) -> dict:
    keys = jax.random.split(jax.random.key(seed), 8)
    q_nope = gaussian(keys[0], (TOKENS, HEADS * HD), 1.0, 6.0, ((0, 16), (1, 2)))
    q_rope = draw_q_rope(jax.random.fold_in(keys[7], 71), 0)
    latent = draw_latent(jax.random.fold_in(keys[7], 71), 0)
    doc_ids = jnp.searchsorted(jnp.cumsum(uneven(keys[3], N_SEQ, TOKENS, (HOPS + 1) * TOK_DEV, 2)), jnp.arange(TOKENS), side="right").astype(jnp.int32)
    w_uk = gaussian(keys[4], (LAT, HEADS * HD), LAT ** -0.5, 0.25, ((1, 2),))
    w_uv = gaussian(keys[5], (LAT, HEADS * VD), LAT ** -0.5, 0.25, ((1, 2),))
    w_out = gaussian(keys[6], (HEADS * VD, DOUT), (HEADS * VD // 32) ** -0.5, 0.375, ((0, 2), (1, 16)))
    return dict(q_nope=q_nope, q_rope=q_rope, latent=latent, doc_ids=doc_ids, w_uk=w_uk, w_uv=w_uv, w_out=w_out)


def reference(q_nope, q_rope, latent, doc_ids, w_uk, w_uv, w_out):
    score_scale = 1.0 / math.sqrt(HD + ROPE)
    content = latent[:, :LAT]
    key_nope = jnp.dot(content, w_uk, preferred_element_type=jnp.float32).astype(jnp.bfloat16)
    values = jnp.dot(content, w_uv, preferred_element_type=jnp.float32).astype(jnp.bfloat16)
    key_rope = latent[:, LAT:]
    reach_back = HOPS * TOK_DEV
    key_span = (HOPS + 1) * TOK_DEV
    nope_padded = jnp.pad(key_nope, ((reach_back, 0), (0, 0)))
    rope_padded = jnp.pad(key_rope, ((reach_back, 0), (0, 0)))
    value_padded = jnp.pad(values, ((reach_back, 0), (0, 0)))
    doc_padded = jnp.pad(doc_ids, (reach_back, 0), constant_values=-1)

    def one_block(block_index):
        offset = (block_index * TOK_DEV).astype(jnp.int32)
        query_nope = lax.dynamic_slice_in_dim(q_nope, offset, TOK_DEV, 0).astype(jnp.float32).reshape(TOK_DEV, HEADS, HD)
        query_rope = lax.dynamic_slice_in_dim(q_rope, offset, TOK_DEV, 0).astype(jnp.float32).reshape(TOK_DEV, HEADS, ROPE)
        block_nope = lax.dynamic_slice_in_dim(nope_padded, offset, key_span, 0).astype(jnp.float32).reshape(key_span, HEADS, HD)
        block_rope = lax.dynamic_slice_in_dim(rope_padded, offset, key_span, 0).astype(jnp.float32)
        block_values = lax.dynamic_slice_in_dim(value_padded, offset, key_span, 0).astype(jnp.float32).reshape(key_span, HEADS, VD)
        query_doc = lax.dynamic_slice_in_dim(doc_ids, offset, TOK_DEV, 0)
        key_doc = lax.dynamic_slice_in_dim(doc_padded, offset, key_span, 0)
        query_pos = offset + jnp.arange(TOK_DEV, dtype=jnp.int32)
        key_pos = offset - reach_back + jnp.arange(key_span, dtype=jnp.int32)
        distance = query_pos[:, None] - key_pos[None, :]
        allowed = (key_pos[None, :] >= 0) & (distance >= 0) & (distance < reach_back) & (query_doc[:, None] == key_doc[None, :])
        scores = (jnp.einsum('qhd,khd->hqk', query_nope, block_nope) + jnp.einsum('qhd,kd->hqk', query_rope, block_rope)) * score_scale
        scores = jnp.where(allowed[None], scores, jnp.float32(-1e+30))
        row_max = lax.optimization_barrier(jnp.max(scores, axis=-1, keepdims=True))
        raw_weights = jnp.where(allowed[None], jnp.exp(scores - row_max), jnp.float32(0.0))
        weights_half = (raw_weights / lax.optimization_barrier(jnp.sum(raw_weights, axis=-1, keepdims=True))).astype(jnp.bfloat16)
        attended = jnp.einsum('hqk,khd->qhd', weights_half.astype(jnp.float32), block_values)
        return attended.astype(jnp.bfloat16).reshape(TOK_DEV, HEADS * VD)
    blocks = lax.map(one_block, jnp.arange(N_SEQ, dtype=jnp.int32))
    attended_all = blocks.reshape(TOKENS, HEADS * VD)
    return jnp.dot(attended_all, w_out, preferred_element_type=jnp.float32).astype(jnp.bfloat16)
```

```python
import functools
import math

import jax
import jax.numpy as jnp
from jax import lax
from jax.experimental import pallas as pl
from jax.experimental.pallas import tpu as pltpu
from jax.sharding import PartitionSpec as P

HD = 128
ROPE = 64
VD = 128
LAT = 512
HOPS = 4
MARKS = 64
FAR = 1e30
PLANE = 4
SLICES = (64, 64, 48, 32, 16)
MESH = pl.DeviceIdType.MESH


def from_behind(value, steps):
    count = lax.axis_size("seq")
    return lax.ppermute(value, "seq", [(source, source + steps) for source in range(count - steps)])


def pair_of_heads(rows, q_nope, q_rope, q_mark, content, tails, w_uk, w_uv):
    scale = math.log2(math.e) / math.sqrt(HD + ROPE)
    keys = content.shape[0]
    key_pair = jnp.dot(content, w_uk, preferred_element_type=jnp.float32).astype(jnp.bfloat16)
    value_pair = jnp.dot(content, w_uv, preferred_element_type=jnp.float32).astype(jnp.bfloat16)
    causal = lax.broadcasted_iota(jnp.int32, (rows, rows), 1) <= lax.broadcasted_iota(jnp.int32, (rows, rows), 0)
    low = lax.broadcasted_iota(jnp.int32, (rows, 2 * ROPE), 1) < ROPE
    ones = jnp.ones((keys, VD), jnp.bfloat16)
    results = []
    for half in range(2):
        cols = slice(half * HD, (half + 1) * HD)
        rope = jnp.where(low == (half == 0), q_rope, q_mark)
        query = jnp.concatenate([q_nope[:, cols], rope], axis=1)
        key = jnp.concatenate([key_pair[:, cols], tails[half]], axis=1)
        scores = lax.dot_general(query, key, (((1,), (1,)), ((), ())), preferred_element_type=jnp.float32)
        edge = jnp.where(causal, scores[:, keys - rows :], scores[:, :rows])
        joined = jnp.concatenate([edge, scores[:, rows : keys - rows]], axis=1)
        top = jnp.max(joined, axis=-1, keepdims=True)
        raw = jnp.exp2((joined - top) * scale).astype(jnp.bfloat16)
        near = jnp.where(causal, raw[:, :rows], jnp.bfloat16(0))
        far = jnp.where(causal, jnp.bfloat16(0), raw[:, :rows])
        weights = jnp.concatenate([far, raw[:, rows:], near], axis=1)
        value = jnp.concatenate([value_pair[:, cols], ones], axis=1)
        total = jnp.dot(weights, value, preferred_element_type=jnp.float32)
        results.append((total[:, :VD] / total[:, VD:]).astype(jnp.bfloat16))
    return jnp.concatenate(results, axis=1)


def attend(rows, q_nope, q_rope, q_mark, content, tails, w_uk, w_uv, out):
    out[...] = pair_of_heads(
        rows, q_nope[...], q_rope[...], q_mark[...], content[...], (tails[0], tails[1]), w_uk[...], w_uv[...]
    )


def attention(q_nope, q_rope, q_mark, content, tails, w_uk, w_uv):
    rows, width = q_nope.shape
    keys = content.shape[0]
    pairs = width // (2 * HD)
    whole = lambda *shape: pl.BlockSpec(shape, lambda i: (0,) * len(shape))
    return pl.pallas_call(
        functools.partial(attend, rows),
        out_shape=jax.ShapeDtypeStruct((rows, width), jnp.bfloat16),
        grid=(pairs,),
        in_specs=[
            pl.BlockSpec((rows, 2 * HD), lambda i: (0, i)),
            pl.BlockSpec((rows, 2 * ROPE), lambda i: (0, i)),
            whole(rows, 2 * ROPE),
            whole(keys, LAT),
            whole(2, keys, 2 * ROPE),
            pl.BlockSpec((LAT, 2 * HD), lambda i: (0, i)),
            pl.BlockSpec((LAT, 2 * HD), lambda i: (0, i)),
        ],
        out_specs=pl.BlockSpec((rows, 2 * VD), lambda i: (0, i)),
        compiler_params=pltpu.CompilerParams(
            dimension_semantics=("arbitrary",), vmem_limit_bytes=48 << 20
        ),
        cost_estimate=pl.CostEstimate(
            flops=pairs * 2 * keys * (2 * LAT * 2 * HD + 4 * rows * 2 * HD),
            bytes_accessed=2 * (rows * width * 3 + LAT * width * 2),
            transcendentals=pairs * 2 * rows * keys,
        ),
        name="attention",
    )(q_nope, q_rope, q_mark, content, tails, w_uk, w_uv)


def shards(q_nope, q_rope, latent, doc_ids, w_uk, w_uv, w_out):
    count, heads = lax.axis_size("seq"), lax.axis_size("head")
    position = lax.axis_index("seq")
    w_rows = w_out.T
    marks = (doc_ids[:, None] == jnp.arange(MARKS, dtype=jnp.int32)[None, :]).astype(jnp.bfloat16)
    payload = jnp.concatenate([latent, marks], axis=1)
    q_mark = (marks - jnp.bfloat16(1)) * jnp.bfloat16(FAR)
    q_mark = jnp.concatenate([q_mark, q_mark], axis=1)
    if count == 4 * PLANE and heads == 2:
        return fused(q_nope, q_rope, q_mark, payload, w_uk, w_uv, w_rows)
    blocks = []
    for distance in range(HOPS, 0, -1):
        block = from_behind(payload, distance)
        blocks.append(
            jnp.concatenate(
                [block[:, : LAT + ROPE], jnp.where(position >= distance, block[:, LAT + ROPE :], jnp.bfloat16(1))],
                axis=1,
            )
        )
    blocks.append(payload)
    behind = jnp.concatenate(blocks, axis=0)
    content = behind[:, :LAT]
    key_rope, key_marks = behind[:, LAT : LAT + ROPE], behind[:, LAT + ROPE :]
    tails = jnp.stack(
        [jnp.concatenate([key_rope, key_marks], axis=1), jnp.concatenate([key_marks, key_rope], axis=1)]
    )
    fixed = (q_mark, content, tails)
    attended = attention(q_nope, q_rope, *fixed, w_uk, w_uv)
    whole = lax.all_gather(w_rows, "seq", axis=0, tiled=True)
    share = product(attended, whole)
    return lax.psum_scatter(share, "head", scatter_dimension=1, tiled=True).astype(jnp.bfloat16)


def product(left, right):
    return lax.dot_general(left, right, (((1,), (1,)), ((), ())), preferred_element_type=jnp.float32)


def whole_layer(
    q_nope, q_rope, q_mark, payload, w_uk, w_uv, w_rows, out,
    qn, qr, qm, uk, uv, halo, turned, near_w, far_w, tokens, give, taken, kept, done,
    load_sem, halo_out, halo_in, near_out, near_in, far_out, far_in, pass_out, pass_in,
    token_out, token_in, share_out, share_in, result_out, result_in,
):
    rows, width = q_nope.shape
    slab = w_rows.shape[0]
    pairs = width // (2 * HD)
    slices = [(sum(SLICES[:i]), size) for i, size in enumerate(SLICES)]
    me, side = lax.axis_index("seq"), lax.axis_index("head")
    plane, row, core = me // PLANE, (me // 2) % 2, me % 2
    parity = plane % 2
    beyond = me + 4 * (1 - 2 * parity)
    mate = me + 1 - 2 * core
    across = me + 2 - 4 * row
    beyond_mate = mate + 4 * (1 - 2 * parity)
    opposite = me + 4 * (3 - 2 * plane)
    here = lambda seq: (seq, side)
    twin = (me, 1 - side)
    inner = (plane == 1) | (plane == 2)
    outer = jnp.logical_not(inner)
    keeps_near = side == plane // 2
    keeps_far = jnp.logical_not(keeps_near)

    def remote(source, target, out_sem, in_sem, device):
        return pltpu.make_async_remote_copy(
            src_ref=source, dst_ref=target, send_sem=out_sem, recv_sem=in_sem, device_id=device, device_id_type=MESH
        )

    partners = [here(beyond), here(mate), here(across), here(beyond_mate), here(opposite), twin]
    barrier = pltpu.get_barrier_semaphore()
    for partner in partners:
        pl.semaphore_signal(barrier, inc=1, device_id=partner, device_id_type=MESH)
    loads = [
        pltpu.make_async_copy(source, target, load_sem.at[i])
        for i, (source, target) in enumerate(
            [(payload, halo.at[pl.ds(HOPS * rows, rows)]), (q_mark, qm), (w_uk, uk), (w_uv, uv), (q_nope, qn), (q_rope, qr)]
            + [(w_rows, near_w.at[row])]
        )
    ]
    for load in loads:
        load.start()
    pl.semaphore_wait(barrier, len(partners))

    slot = lambda i: halo.at[pl.ds(pl.multiple_of(i * rows, rows), rows)]
    step_behind = remote(payload, slot(0), halo_out.at[0], halo_in.at[0], here(me + PLANE))
    step_across = lambda source: remote(source, slot(2), halo_out.at[1], halo_in.at[1], here(across))
    step_mate = lambda source: remote(source, slot(3 - 2 * core), halo_out.at[2], halo_in.at[2], here(mate))
    step_second = remote(slot(2), slot(1 + 2 * core), halo_out.at[3], halo_in.at[3], here(mate))
    pl.when(plane < 3)(step_behind.start)
    pl.when(row == 0)(step_across(payload).start)
    pl.when(core == 0)(step_mate(payload).start)

    def far_copy(i):
        start, size = slices[i]
        part = pl.ds(start, size)
        return remote(w_rows.at[part], far_w.at[row, part], far_out.at[i], far_in.at[i], here(opposite))

    def pass_copy(i):
        start, size = slices[i]
        part = far_w.at[row, pl.ds(start, size)]
        return remote(part, part, pass_out.at[i], pass_in.at[i], here(across))

    def pass_wait(i):
        start, size = slices[i]
        part = far_w.at[1 - row, pl.ds(start, size)]
        remote(part, part, pass_out.at[i], pass_in.at[i], here(across)).wait_recv()

    far_copy(0).start()

    @pl.when(inner)
    def _():
        for i in range(1, len(slices)):
            far_copy(i).start()

    @pl.when(plane == 0)
    def _():
        lanes = lax.broadcasted_iota(jnp.int32, (rows, halo.shape[1]), 1)
        halo[:rows] = jnp.where(lanes < LAT + ROPE, 0.0, 1.0).astype(jnp.bfloat16)

    pl.when(plane > 0)(step_behind.wait_recv)
    pl.when(row == 1)(step_across(slot(0)).start)
    pl.when(core == 1)(step_mate(slot(0)).start)
    near_copy = remote(w_rows, near_w.at[row], near_out.at[0], near_in.at[0], here(across))
    near_copy.start()
    step_across(slot(0)).wait_recv()
    step_second.start()
    step_mate(slot(0)).wait_recv()
    step_second.wait_recv()
    for load in loads:
        load.wait()
    tail = halo[:, LAT:].astype(jnp.float32)
    turned[...] = pltpu.roll(tail, ROPE, 1).astype(jnp.bfloat16)

    def columns(i):
        return pl.ds(pl.multiple_of(i * 2 * HD, 2 * HD), 2 * HD)

    def token_copy(kind, i):
        source, target, device = [(0, 1, mate), (0, 2, beyond), (2, 3, mate)][kind]
        return remote(
            tokens.at[source, :, columns(i)],
            tokens.at[target, :, columns(i)],
            token_out.at[kind, i],
            token_in.at[kind, i],
            here(device),
        )

    def relay(i):
        token_copy(1, i).wait_recv()
        token_copy(2, i).start()

    def heads(i, carry):
        tokens[0, :, columns(i)] = pair_of_heads(
            rows,
            qn[:, columns(i)],
            qr[:, pl.ds(pl.multiple_of(i * 2 * ROPE, 2 * ROPE), 2 * ROPE)],
            qm[...],
            halo[:, :LAT],
            (halo[:, LAT:], turned[...]),
            uk[:, columns(i)],
            uv[:, columns(i)],
        )
        token_copy(1, i).start()
        token_copy(0, i).start()

        @pl.when(i % 2 == 1)
        def _():
            relay(i // 2)

        return carry

    lax.fori_loop(0, pairs, heads, 0)

    @pl.when(outer)
    def _():
        for i in range(1, len(slices)):
            far_copy(i).start()

    def forward(i):
        far_copy(i).wait_recv()
        pass_copy(i).start()

    forward(0)

    @pl.when(inner)
    def _():
        for i in range(1, len(slices)):
            forward(i)

    def all_pairs(step):
        def body(i, carry):
            step(i)
            return carry

        return body

    def share_copy(i, blocks, part):
        where = (pl.ds(*blocks), slice(None), pl.ds(*part))
        return remote(give.at[where], taken.at[where], share_out.at[i], share_in.at[i], twin)

    def near_block(b, carry):
        share = product(near_w[...].reshape(2 * slab, width), tokens[b]).reshape(2, slab, rows)

        @pl.when(keeps_near)
        def _():
            kept[b] = share

        @pl.when(keeps_far)
        def _():
            give[b] = share.astype(jnp.bfloat16)

        return carry

    whole = (0, slab)
    near_copy_back = remote(w_rows, near_w.at[1 - row], near_out.at[0], near_in.at[0], here(across))
    near_copy_back.wait_recv()
    lax.fori_loop(0, pairs, all_pairs(lambda i: token_copy(0, i).wait_recv()), 0)
    lax.fori_loop(0, 2, near_block, 0)
    pl.when(keeps_far)(share_copy(0, (0, 2), whole).start)
    lax.fori_loop(pairs // 2, pairs, all_pairs(relay), 0)
    lax.fori_loop(0, pairs, all_pairs(lambda i: token_copy(2, i).wait_recv()), 0)
    lax.fori_loop(2, 4, near_block, 0)
    pl.when(keeps_far)(share_copy(1, (2, 2), whole).start)

    def result_copy(b, unit, part, group):
        start, size = part
        target = out.at[group, :, core, pl.ds(start, size), :]
        source = done.at[b, :, pl.ds(start, size), :]
        if b == 0:
            return pltpu.make_async_copy(source, target, result_out.at[b, unit])
        device = here([mate, beyond, beyond_mate][b - 1])
        return remote(source, target, result_out.at[b, unit], result_in.at[b - 1, unit], device)

    def finish(i, unit, blocks, part, group):
        share_copy(i, blocks, part).wait_recv()
        first, count = blocks
        where = pl.ds(*part)
        for b in range(first, first + count):
            done[b, :, where, :] = (kept[b, :, where, :] + taken[b, :, where, :].astype(jnp.float32)).astype(jnp.bfloat16)
            result_copy(b, unit, part, group).start()

    @pl.when(keeps_near)
    def _():
        finish(0, 0, (0, 2), whole, parity)
        finish(1, 0, (2, 2), whole, parity)

    def far_block(part):
        start, size = part

        def body(b, carry):
            share = product(far_w[:, pl.ds(start, size), :].reshape(2 * size, width), tokens[b]).reshape(2, size, rows)

            @pl.when(keeps_far)
            def _():
                kept[b, :, pl.ds(start, size), :] = share

            @pl.when(keeps_near)
            def _():
                give[b, :, pl.ds(start, size), :] = share.astype(jnp.bfloat16)

            return carry

        return body

    def finish_far(i):
        finish(2 + i, 1 + i, (0, 4), slices[i], 1 - parity)

    for i, part in enumerate(slices):
        if i + 1 < len(slices):
            pl.when(outer)(functools.partial(forward, i + 1))
        pass_wait(i)
        lax.fori_loop(0, 4, far_block(part), 0)
        pl.when(keeps_near)(share_copy(2 + i, (0, 4), part).start)
        if i > 0:
            pl.when(keeps_far)(functools.partial(finish_far, i - 1))
    pl.when(keeps_far)(functools.partial(finish_far, len(slices) - 1))

    def settle(units, group):
        for unit, part, blocks in units:
            for b in blocks:
                copy = result_copy(b, unit, part, group)
                if b == 0:
                    copy.wait()
                else:
                    copy.wait_send()
                    copy.wait_recv()

    @pl.when(keeps_near)
    def _():
        settle([(0, whole, range(4))], parity)
        for i, part in enumerate(slices):
            share_copy(2 + i, (0, 4), part).wait_send()

    @pl.when(keeps_far)
    def _():
        settle([(1 + i, part, range(4)) for i, part in enumerate(slices)], 1 - parity)
        share_copy(0, (0, 2), whole).wait_send()
        share_copy(1, (2, 2), whole).wait_send()

    pl.when(plane < 3)(step_behind.wait_send)
    step_across(slot(0)).wait_send()
    step_mate(slot(0)).wait_send()
    step_second.wait_send()
    near_copy.wait_send()
    for i in range(len(slices)):
        far_copy(i).wait_send()
        pass_copy(i).wait_send()
    for kind in range(3):
        lax.fori_loop(0, pairs, all_pairs(lambda i, kind=kind: token_copy(kind, i).wait_send()), 0)


def fused(q_nope, q_rope, q_mark, payload, w_uk, w_uv, w_rows):
    rows, width = q_nope.shape
    slab = w_rows.shape[0]
    keys = (HOPS + 1) * rows
    pairs = width // (2 * HD)
    count = len(SLICES)
    assert sum(SLICES) == slab
    half = jnp.bfloat16
    copies = lambda *shape: pltpu.SemaphoreType.DMA(shape)
    result = pl.pallas_call(
        whole_layer,
        out_shape=jax.ShapeDtypeStruct((2, 2, 2, slab, rows), half),
        in_specs=[pl.BlockSpec(memory_space=pl.ANY)] * 7,
        out_specs=pl.BlockSpec(memory_space=pl.ANY),
        scratch_shapes=[
            pltpu.VMEM(q_nope.shape, half),
            pltpu.VMEM(q_rope.shape, half),
            pltpu.VMEM(q_mark.shape, half),
            pltpu.VMEM(w_uk.shape, half),
            pltpu.VMEM(w_uv.shape, half),
            pltpu.VMEM((keys, payload.shape[1]), half),
            pltpu.VMEM((keys, 2 * ROPE), half),
            pltpu.VMEM((2, slab, width), half),
            pltpu.VMEM((2, slab, width), half),
            pltpu.VMEM((4, rows, width), half),
            pltpu.VMEM((4, 2, slab, rows), half),
            pltpu.VMEM((4, 2, slab, rows), half),
            pltpu.VMEM((4, 2, slab, rows), jnp.float32),
            pltpu.VMEM((4, 2, slab, rows), half),
            copies(7), copies(4), copies(4), copies(1), copies(1), copies(count), copies(count), copies(count), copies(count),
            copies(3, pairs), copies(3, pairs), copies(2 + count), copies(2 + count), copies(4, 1 + count), copies(3, 1 + count),
        ],
        compiler_params=pltpu.CompilerParams(
            collective_id=0, has_side_effects=True, vmem_limit_bytes=56 << 20
        ),
        name="whole_layer",
    )(q_nope, q_rope, q_mark, payload, w_uk, w_uv, w_rows)
    return result.reshape(8 * slab, rows).T


def solution(mesh):
    placed = (
        P("seq", "head"),
        P("seq", "head"),
        P("seq", None),
        P("seq"),
        P(None, "head"),
        P(None, "head"),
        P("head", "seq"),
    )
    return jax.shard_map(
        shards, mesh=mesh, in_specs=placed, out_specs=P("seq", "head"), check_vma=False
    )
```

```python
import functools
import math

import jax
import jax.numpy as jnp
from jax import lax
from jax.experimental import pallas as pl
from jax.experimental.pallas import tpu as pltpu
from jax.sharding import PartitionSpec as P

HD = 128
ROPE = 64
VD = 128
LAT = 512
HOPS = 4
MARKS = 64
FAR = 1e30
PLANE = 4
SLICES = (80, 32, 32, 32, 32, 16)
GROUPS = ((0, 0), (1, 2), (3, 4), (5, 5))
MESH = pl.DeviceIdType.MESH


def from_behind(value, steps):
    count = lax.axis_size("seq")
    return lax.ppermute(value, "seq", [(source, source + steps) for source in range(count - steps)])


def pair_of_heads(rows, q_nope, q_rope, q_mark, content, tails, w_uk, w_uv):
    scale = math.log2(math.e) / math.sqrt(HD + ROPE)
    keys = content.shape[0]
    key_pair = jnp.dot(content, w_uk, preferred_element_type=jnp.float32).astype(jnp.bfloat16)
    value_pair = jnp.dot(content, w_uv, preferred_element_type=jnp.float32).astype(jnp.bfloat16)
    causal = lax.broadcasted_iota(jnp.int32, (rows, rows), 1) <= lax.broadcasted_iota(jnp.int32, (rows, rows), 0)
    low = lax.broadcasted_iota(jnp.int32, (rows, 2 * ROPE), 1) < ROPE
    ones = jnp.ones((keys, VD), jnp.bfloat16)
    results = []
    for half in range(2):
        cols = slice(half * HD, (half + 1) * HD)
        rope = jnp.where(low == (half == 0), q_rope, q_mark)
        query = jnp.concatenate([q_nope[:, cols], rope], axis=1)
        key = jnp.concatenate([key_pair[:, cols], tails[half]], axis=1)
        scores = lax.dot_general(query, key, (((1,), (1,)), ((), ())), preferred_element_type=jnp.float32)
        edge = jnp.where(causal, scores[:, keys - rows :], scores[:, :rows])
        joined = jnp.concatenate([edge, scores[:, rows : keys - rows]], axis=1)
        top = jnp.max(joined, axis=-1, keepdims=True)
        raw = jnp.exp2((joined - top) * scale).astype(jnp.bfloat16)
        near = jnp.where(causal, raw[:, :rows], jnp.bfloat16(0))
        far = jnp.where(causal, jnp.bfloat16(0), raw[:, :rows])
        weights = jnp.concatenate([far, raw[:, rows:], near], axis=1)
        value = jnp.concatenate([value_pair[:, cols], ones], axis=1)
        total = jnp.dot(weights, value, preferred_element_type=jnp.float32)
        results.append((total[:, :VD] / total[:, VD:]).astype(jnp.bfloat16))
    return jnp.concatenate(results, axis=1)


def attend(rows, q_nope, q_rope, q_mark, content, tails, w_uk, w_uv, out):
    out[...] = pair_of_heads(
        rows, q_nope[...], q_rope[...], q_mark[...], content[...], (tails[0], tails[1]), w_uk[...], w_uv[...]
    )


def attention(q_nope, q_rope, q_mark, content, tails, w_uk, w_uv):
    rows, width = q_nope.shape
    keys = content.shape[0]
    pairs = width // (2 * HD)
    whole = lambda *shape: pl.BlockSpec(shape, lambda i: (0,) * len(shape))
    return pl.pallas_call(
        functools.partial(attend, rows),
        out_shape=jax.ShapeDtypeStruct((rows, width), jnp.bfloat16),
        grid=(pairs,),
        in_specs=[
            pl.BlockSpec((rows, 2 * HD), lambda i: (0, i)),
            pl.BlockSpec((rows, 2 * ROPE), lambda i: (0, i)),
            whole(rows, 2 * ROPE),
            whole(keys, LAT),
            whole(2, keys, 2 * ROPE),
            pl.BlockSpec((LAT, 2 * HD), lambda i: (0, i)),
            pl.BlockSpec((LAT, 2 * HD), lambda i: (0, i)),
        ],
        out_specs=pl.BlockSpec((rows, 2 * VD), lambda i: (0, i)),
        compiler_params=pltpu.CompilerParams(
            dimension_semantics=("arbitrary",), vmem_limit_bytes=48 << 20
        ),
        cost_estimate=pl.CostEstimate(
            flops=pairs * 2 * keys * (2 * LAT * 2 * HD + 4 * rows * 2 * HD),
            bytes_accessed=2 * (rows * width * 3 + LAT * width * 2),
            transcendentals=pairs * 2 * rows * keys,
        ),
        name="attention",
    )(q_nope, q_rope, q_mark, content, tails, w_uk, w_uv)


def shards(q_nope, q_rope, latent, doc_ids, w_uk, w_uv, w_out):
    count, heads = lax.axis_size("seq"), lax.axis_size("head")
    position = lax.axis_index("seq")
    w_rows = w_out.T
    marks = (doc_ids[:, None] == jnp.arange(MARKS, dtype=jnp.int32)[None, :]).astype(jnp.bfloat16)
    if count == 4 * PLANE and heads == 2:
        return fused(q_nope, q_rope, latent.T, doc_ids[None, :], w_uk, w_uv, w_rows)
    payload = jnp.concatenate([latent, marks], axis=1)
    q_mark = (marks - jnp.bfloat16(1)) * jnp.bfloat16(FAR)
    q_mark = jnp.concatenate([q_mark, q_mark], axis=1)
    blocks = []
    for distance in range(HOPS, 0, -1):
        block = from_behind(payload, distance)
        blocks.append(
            jnp.concatenate(
                [block[:, : LAT + ROPE], jnp.where(position >= distance, block[:, LAT + ROPE :], jnp.bfloat16(1))],
                axis=1,
            )
        )
    blocks.append(payload)
    behind = jnp.concatenate(blocks, axis=0)
    content = behind[:, :LAT]
    key_rope, key_marks = behind[:, LAT : LAT + ROPE], behind[:, LAT + ROPE :]
    tails = jnp.stack(
        [jnp.concatenate([key_rope, key_marks], axis=1), jnp.concatenate([key_marks, key_rope], axis=1)]
    )
    fixed = (q_mark, content, tails)
    attended = attention(q_nope, q_rope, *fixed, w_uk, w_uv)
    whole = lax.all_gather(w_rows, "seq", axis=0, tiled=True)
    share = product(attended, whole)
    return lax.psum_scatter(share, "head", scatter_dimension=1, tiled=True).astype(jnp.bfloat16)


def product(left, right):
    return lax.dot_general(left, right, (((1,), (1,)), ((), ())), preferred_element_type=jnp.float32)


def whole_layer(
    q_nope, q_rope, latent, doc_ids, w_uk, w_uv, w_rows, out,
    qn, qr, raw, qm, uk, uv, halo, turned, near_w, far_w, tokens, give, taken, kept, done,
    load_sem, halo_out, halo_in, near_out, near_in, far_out, far_in, pass_out, pass_in,
    token_out, token_in, share_out, share_in, result_out, result_in,
):
    rows, width = q_nope.shape
    slab = w_rows.shape[0]
    pairs = width // (2 * HD)
    slices = [(sum(SLICES[:i]), size) for i, size in enumerate(SLICES)]
    me, side = lax.axis_index("seq"), lax.axis_index("head")
    plane, row, core = me // PLANE, (me // 2) % 2, me % 2
    parity = plane % 2
    beyond = me + 4 * (1 - 2 * parity)
    mate = me + 1 - 2 * core
    across = me + 2 - 4 * row
    beyond_mate = mate + 4 * (1 - 2 * parity)
    opposite = me + 4 * (3 - 2 * plane)
    here = lambda seq: (seq, side)
    twin = (me, 1 - side)
    inner = (plane == 1) | (plane == 2)
    outer = jnp.logical_not(inner)
    keeps_near = side == plane // 2
    keeps_far = jnp.logical_not(keeps_near)

    def remote(source, target, out_sem, in_sem, device):
        return pltpu.make_async_remote_copy(
            src_ref=source, dst_ref=target, send_sem=out_sem, recv_sem=in_sem, device_id=device, device_id_type=MESH
        )

    partners = [here(beyond), here(mate), here(across), here(beyond_mate), here(opposite), twin]
    barrier = pltpu.get_barrier_semaphore()
    for partner in partners:
        pl.semaphore_signal(barrier, inc=1, device_id=partner, device_id_type=MESH)
    loads = [
        pltpu.make_async_copy(source, target, load_sem.at[i])
        for i, (source, target) in enumerate(
            [(latent, raw), (w_uk, uk), (w_uv, uv), (q_nope, qn), (q_rope, qr), (w_rows, near_w.at[row])]
        )
    ]
    for load in loads:
        load.start()
    kinds = lax.broadcasted_iota(jnp.int32, (2 * MARKS, rows), 0) % MARKS
    marks = jnp.where(kinds == doc_ids[...], 1.0, 0.0).astype(jnp.float32)
    qm[...] = ((marks - 1.0) * FAR).T.astype(jnp.bfloat16)
    loads[0].wait()
    halo[HOPS * rows :] = jnp.concatenate([raw[...].astype(jnp.float32), marks[:MARKS]], axis=0).T.astype(jnp.bfloat16)
    pl.semaphore_wait(barrier, len(partners))

    half = rows // 2

    def slot(i, part):
        return halo.at[pl.ds(pl.multiple_of(i * rows + (part ^ side) * half, half), half)]

    def step_behind(part):
        return remote(slot(HOPS, part), slot(0, part), halo_out.at[0, part], halo_in.at[0, part], here(me + PLANE))

    def step_twin(part):
        return remote(slot(0, part), slot(0, part), halo_out.at[0, 1], halo_in.at[0, 1], twin)

    def step_across(source, part):
        return remote(slot(source, part), slot(2, part), halo_out.at[1, part], halo_in.at[1, part], here(across))

    def step_mate(source, part):
        return remote(slot(source, part), slot(3 - 2 * core, part), halo_out.at[2, part], halo_in.at[2, part], here(mate))

    def step_second(part):
        return remote(slot(2, part), slot(1 + 2 * core, part), halo_out.at[3, part], halo_in.at[3, part], here(mate))

    def mate_wait(part):
        remote(slot(0, part), slot(1 + 2 * core, part), halo_out.at[2, part], halo_in.at[2, part], here(mate)).wait_recv()

    def second_wait(part):
        remote(slot(2, part), slot(3 - 2 * core, part), halo_out.at[3, part], halo_in.at[3, part], here(mate)).wait_recv()

    pl.when(plane < 3)(step_behind(0).start)
    for part in range(2):
        pl.when(row == 0)(step_across(HOPS, part).start)
        pl.when(core == 0)(step_mate(HOPS, part).start)

    def far_copy(i):
        start, size = slices[i]
        part = pl.ds(start, size)
        return remote(w_rows.at[part], far_w.at[row, part], far_out.at[i], far_in.at[i], here(opposite))

    def pass_copy(i):
        start, size = slices[i]
        part = far_w.at[row, pl.ds(start, size)]
        return remote(part, part, pass_out.at[i], pass_in.at[i], here(across))

    def pass_wait(i):
        start, size = slices[i]
        part = far_w.at[1 - row, pl.ds(start, size)]
        remote(part, part, pass_out.at[i], pass_in.at[i], here(across)).wait_recv()

    far_copy(0).start()

    @pl.when(inner)
    def _():
        for i in range(1, len(slices)):
            far_copy(i).start()

    @pl.when(plane == 0)
    def _():
        lanes = lax.broadcasted_iota(jnp.int32, (rows, halo.shape[1]), 1)
        halo[:rows] = jnp.where(lanes < LAT + ROPE, 0.0, 1.0).astype(jnp.bfloat16)

    @pl.when(plane > 0)
    def _():
        step_behind(0).wait_recv()
        step_twin(0).start()

    pl.when(row == 1)(step_across(0, 0).start)
    pl.when(core == 1)(step_mate(0, 0).start)

    @pl.when(plane > 0)
    def _():
        step_twin(1).wait_recv()

    pl.when(row == 1)(step_across(0, 1).start)
    pl.when(core == 1)(step_mate(0, 1).start)
    near_copy = remote(w_rows, near_w.at[row], near_out.at[0], near_in.at[0], here(across))
    near_copy.start()
    for part in range(2):
        step_across(0, part).wait_recv()
        step_second(part).start()
    for part in range(2):
        mate_wait(part)
        second_wait(part)
    for load in loads[1:]:
        load.wait()
    tail = halo[:, LAT:].astype(jnp.float32)
    turned[...] = pltpu.roll(tail, ROPE, 1).astype(jnp.bfloat16)

    def columns(i):
        return pl.ds(pl.multiple_of(i * 2 * HD, 2 * HD), 2 * HD)

    def token_copy(kind, i):
        source, target, device = [(0, 1, mate), (0, 2, beyond), (2, 3, mate)][kind]
        return remote(
            tokens.at[source, :, columns(i)],
            tokens.at[target, :, columns(i)],
            token_out.at[kind, i],
            token_in.at[kind, i],
            here(device),
        )

    def relay(i):
        token_copy(1, i).wait_recv()
        token_copy(2, i).start()

    def heads(i, carry):
        tokens[0, :, columns(i)] = pair_of_heads(
            rows,
            qn[:, columns(i)],
            qr[:, pl.ds(pl.multiple_of(i * 2 * ROPE, 2 * ROPE), 2 * ROPE)],
            qm[...],
            halo[:, :LAT],
            (halo[:, LAT:], turned[...]),
            uk[:, columns(i)],
            uv[:, columns(i)],
        )
        token_copy(1, i).start()
        token_copy(0, i).start()

        @pl.when(i % 2 == 1)
        def _():
            relay(i // 2)

        return carry

    lax.fori_loop(0, pairs, heads, 0)

    def forward(i):
        far_copy(i).wait_recv()
        pass_copy(i).start()

    forward(0)

    @pl.when(inner)
    def _():
        for i in range(1, len(slices)):
            forward(i)

    def all_pairs(step):
        def body(i, carry):
            step(i)
            return carry

        return body

    def share_copy(i, blocks, part):
        where = (pl.ds(*blocks), slice(None), pl.ds(*part))
        return remote(give.at[where], taken.at[where], share_out.at[i], share_in.at[i], twin)

    def near_block(b, carry):
        share = product(near_w[...].reshape(2 * slab, width), tokens[b]).reshape(2, slab, rows)

        @pl.when(keeps_near)
        def _():
            kept[b] = share

        @pl.when(keeps_far)
        def _():
            give[b] = share.astype(jnp.bfloat16)

        return carry

    whole = (0, slab)
    near_copy_back = remote(w_rows, near_w.at[1 - row], near_out.at[0], near_in.at[0], here(across))
    near_copy_back.wait_recv()
    lax.fori_loop(0, pairs, all_pairs(lambda i: token_copy(0, i).wait_recv()), 0)
    lax.fori_loop(0, 2, near_block, 0)
    pl.when(keeps_far)(share_copy(0, (0, 2), whole).start)
    lax.fori_loop(pairs // 2, pairs - 2, all_pairs(relay), 0)

    @pl.when(outer)
    def _():
        for i in range(1, len(slices)):
            far_copy(i).start()

    lax.fori_loop(pairs - 2, pairs, all_pairs(relay), 0)
    lax.fori_loop(0, pairs, all_pairs(lambda i: token_copy(2, i).wait_recv()), 0)
    lax.fori_loop(2, 4, near_block, 0)
    pl.when(keeps_far)(share_copy(1, (2, 2), whole).start)

    def result_copy(b, unit, part, group):
        start, size = part
        target = out.at[group, :, core, pl.ds(start, size), :]
        source = done.at[b, :, pl.ds(start, size), :]
        if b == 0:
            return pltpu.make_async_copy(source, target, result_out.at[b, unit])
        device = here([mate, beyond, beyond_mate][b - 1])
        return remote(source, target, result_out.at[b, unit], result_in.at[b - 1, unit], device)

    groups = [(slices[first][0], sum(SLICES[first : last + 1]), range(first, last + 1)) for first, last in GROUPS]

    def add(i, unit, blocks, part, group):
        share_copy(i, blocks, part).wait_recv()
        first, count = blocks
        where = pl.ds(*part)
        for b in range(first, first + count):
            done[b, :, where, :] = (kept[b, :, where, :] + taken[b, :, where, :].astype(jnp.float32)).astype(jnp.bfloat16)
            if b < 2:
                result_copy(b, unit, part, group).start()

    def cross(unit, part, group):
        for b in (2, 3):
            result_copy(b, unit, part, group).start()

    def far_block(part):
        start, size = part

        def body(b, carry):
            share = product(far_w[:, pl.ds(start, size), :].reshape(2 * size, width), tokens[b]).reshape(2, size, rows)

            @pl.when(keeps_far)
            def _():
                kept[b, :, pl.ds(start, size), :] = share

            @pl.when(keeps_near)
            def _():
                give[b, :, pl.ds(start, size), :] = share.astype(jnp.bfloat16)

            return carry

        return body

    def add_far(g):
        add(2 + g, 1 + g, (0, 4), groups[g][:2], 1 - parity)

    def cross_far(g):
        cross(1 + g, groups[g][:2], 1 - parity)

    def forward_group(g):
        for i in groups[g][2]:
            forward(i)

    last = len(groups) - 1
    for g, (start, size, members) in enumerate(groups):
        if g + 1 <= last:
            @pl.when(outer)
            def _():
                forward(groups[g + 1][2][0])
                if g > 0:
                    for i in groups[g + 1][2][1:]:
                        forward(i)
        for i in members:
            pass_wait(i)
        lax.fori_loop(0, 4, far_block((start, size)), 0)
        pl.when(keeps_near)(share_copy(2 + g, (0, 4), (start, size)).start)
        if g == 0 and last > 0:
            @pl.when(outer)
            def _():
                for i in groups[1][2][1:]:
                    forward(i)
        if g == 1:
            @pl.when(keeps_near)
            def _():
                add(0, 0, (0, 2), whole, parity)
                add(1, 0, (2, 2), whole, parity)

        if g == last - 1:
            pl.when(keeps_near)(functools.partial(cross, 0, whole, parity))

            @pl.when(keeps_far)
            def _():
                for i in range(last - 1):
                    if i == last - 2:
                        add_far(i)
                    cross_far(i)
        elif 0 < g < last:
            pl.when(keeps_far)(functools.partial(add_far, g - 1))

    @pl.when(keeps_far)
    def _():
        for g in range(last - 1, last + 1):
            add_far(g)
            cross_far(g)

    def settle(units, group):
        for unit, part, blocks in units:
            for b in blocks:
                copy = result_copy(b, unit, part, group)
                if b == 0:
                    copy.wait()
                else:
                    copy.wait_send()
                    copy.wait_recv()

    @pl.when(keeps_near)
    def _():
        settle([(0, whole, range(4))], parity)
        for g, (start, size, _) in enumerate(groups):
            share_copy(2 + g, (0, 4), (start, size)).wait_send()

    @pl.when(keeps_far)
    def _():
        settle([(1 + g, (start, size), range(4)) for g, (start, size, _) in enumerate(groups)], 1 - parity)
        share_copy(0, (0, 2), whole).wait_send()
        share_copy(1, (2, 2), whole).wait_send()

    pl.when(plane < 3)(step_behind(0).wait_send)
    pl.when(plane > 0)(step_twin(0).wait_send)
    for part in range(2):
        step_across(0, part).wait_send()
        step_mate(0, part).wait_send()
        step_second(part).wait_send()
    near_copy.wait_send()
    for i in range(len(slices)):
        far_copy(i).wait_send()
        pass_copy(i).wait_send()
    for kind in range(3):
        lax.fori_loop(0, pairs, all_pairs(lambda i, kind=kind: token_copy(kind, i).wait_send()), 0)


def fused(q_nope, q_rope, latent, doc_ids, w_uk, w_uv, w_rows):
    rows, width = q_nope.shape
    slab = w_rows.shape[0]
    keys = (HOPS + 1) * rows
    pairs = width // (2 * HD)
    count, units = len(SLICES), len(GROUPS)
    assert sum(SLICES) == slab
    half = jnp.bfloat16
    copies = lambda *shape: pltpu.SemaphoreType.DMA(shape)
    result = pl.pallas_call(
        whole_layer,
        out_shape=jax.ShapeDtypeStruct((2, 2, 2, slab, rows), half),
        in_specs=[pl.BlockSpec(memory_space=pltpu.VMEM if i == 3 else pl.ANY) for i in range(7)],
        out_specs=pl.BlockSpec(memory_space=pl.ANY),
        scratch_shapes=[
            pltpu.VMEM(q_nope.shape, half),
            pltpu.VMEM(q_rope.shape, half),
            pltpu.VMEM(latent.shape, half),
            pltpu.VMEM((rows, 2 * MARKS), half),
            pltpu.VMEM(w_uk.shape, half),
            pltpu.VMEM(w_uv.shape, half),
            pltpu.VMEM((keys, latent.shape[0] + MARKS), half),
            pltpu.VMEM((keys, 2 * ROPE), half),
            pltpu.VMEM((2, slab, width), half),
            pltpu.VMEM((2, slab, width), half),
            pltpu.VMEM((4, rows, width), half),
            pltpu.VMEM((4, 2, slab, rows), half),
            pltpu.VMEM((4, 2, slab, rows), half),
            pltpu.VMEM((4, 2, slab, rows), jnp.float32),
            pltpu.VMEM((4, 2, slab, rows), half),
            copies(6), copies(4, 2), copies(4, 2), copies(1), copies(1), copies(count), copies(count), copies(count), copies(count),
            copies(3, pairs), copies(3, pairs), copies(2 + units), copies(2 + units), copies(4, 1 + units), copies(3, 1 + units),
        ],
        compiler_params=pltpu.CompilerParams(
            collective_id=0, has_side_effects=True, vmem_limit_bytes=56 << 20
        ),
        name="whole_layer",
    )(q_nope, q_rope, latent, doc_ids, w_uk, w_uv, w_rows)
    return result.reshape(8 * slab, rows).T


def solution(mesh):
    placed = (
        P("seq", "head"),
        P("seq", "head"),
        P("seq", None),
        P("seq"),
        P(None, "head"),
        P(None, "head"),
        P("head", "seq"),
    )
    return jax.shard_map(
        shards, mesh=mesh, in_specs=placed, out_specs=P("seq", "head"), check_vma=False
    )
```

```python
import functools
import math

import jax
import jax.numpy as jnp
from jax import lax
from jax.experimental import pallas as pl
from jax.experimental.pallas import tpu as pltpu
from jax.sharding import PartitionSpec as P

HD = 128
ROPE = 64
VD = 128
LAT = 512
HOPS = 4
MARKS = 64
FAR = 1e30
PLANE = 4
SLICES = (96, 16, 16, 16, 16, 16, 16, 16, 16)
GROUPS = ((0, 0), (1, 3), (4, 6), (7, 8))
BITS = 2
MESH = pl.DeviceIdType.MESH


def from_behind(value, steps):
    count = lax.axis_size("seq")
    return lax.ppermute(value, "seq", [(source, source + steps) for source in range(count - steps)])


def pair_of_heads(rows, q_nope, q_rope, q_mark, content, tails, w_uk, w_uv):
    scale = math.log2(math.e) / math.sqrt(HD + ROPE)
    keys = content.shape[0]
    key_pair = jnp.dot(content, w_uk, preferred_element_type=jnp.float32).astype(jnp.bfloat16)
    value_pair = jnp.dot(content, w_uv, preferred_element_type=jnp.float32).astype(jnp.bfloat16)
    causal = lax.broadcasted_iota(jnp.int32, (rows, rows), 1) <= lax.broadcasted_iota(jnp.int32, (rows, rows), 0)
    low = lax.broadcasted_iota(jnp.int32, (rows, 2 * ROPE), 1) < ROPE
    ones = jnp.ones((keys, VD), jnp.bfloat16)
    results = []
    for half in range(2):
        cols = slice(half * HD, (half + 1) * HD)
        rope = jnp.where(low == (half == 0), q_rope, q_mark)
        query = jnp.concatenate([q_nope[:, cols], rope], axis=1)
        key = jnp.concatenate([key_pair[:, cols], tails[half]], axis=1)
        scores = lax.dot_general(query, key, (((1,), (1,)), ((), ())), preferred_element_type=jnp.float32)
        edge = jnp.where(causal, scores[:, keys - rows :], scores[:, :rows])
        joined = jnp.concatenate([edge, scores[:, rows : keys - rows]], axis=1)
        top = jnp.max(joined, axis=-1, keepdims=True)
        raw = jnp.exp2((joined - top) * scale).astype(jnp.bfloat16)
        near = jnp.where(causal, raw[:, :rows], jnp.bfloat16(0))
        far = jnp.where(causal, jnp.bfloat16(0), raw[:, :rows])
        weights = jnp.concatenate([far, raw[:, rows:], near], axis=1)
        value = jnp.concatenate([value_pair[:, cols], ones], axis=1)
        total = jnp.dot(weights, value, preferred_element_type=jnp.float32)
        results.append((total[:, :VD] / total[:, VD:]).astype(jnp.bfloat16))
    return jnp.concatenate(results, axis=1)


def attend(rows, q_nope, q_rope, q_mark, content, tails, w_uk, w_uv, out):
    out[...] = pair_of_heads(
        rows, q_nope[...], q_rope[...], q_mark[...], content[...], (tails[0], tails[1]), w_uk[...], w_uv[...]
    )


def attention(q_nope, q_rope, q_mark, content, tails, w_uk, w_uv):
    rows, width = q_nope.shape
    keys = content.shape[0]
    pairs = width // (2 * HD)
    whole = lambda *shape: pl.BlockSpec(shape, lambda i: (0,) * len(shape))
    return pl.pallas_call(
        functools.partial(attend, rows),
        out_shape=jax.ShapeDtypeStruct((rows, width), jnp.bfloat16),
        grid=(pairs,),
        in_specs=[
            pl.BlockSpec((rows, 2 * HD), lambda i: (0, i)),
            pl.BlockSpec((rows, 2 * ROPE), lambda i: (0, i)),
            whole(rows, 2 * ROPE),
            whole(keys, LAT),
            whole(2, keys, 2 * ROPE),
            pl.BlockSpec((LAT, 2 * HD), lambda i: (0, i)),
            pl.BlockSpec((LAT, 2 * HD), lambda i: (0, i)),
        ],
        out_specs=pl.BlockSpec((rows, 2 * VD), lambda i: (0, i)),
        compiler_params=pltpu.CompilerParams(
            dimension_semantics=("arbitrary",), vmem_limit_bytes=48 << 20
        ),
        cost_estimate=pl.CostEstimate(
            flops=pairs * 2 * keys * (2 * LAT * 2 * HD + 4 * rows * 2 * HD),
            bytes_accessed=2 * (rows * width * 3 + LAT * width * 2),
            transcendentals=pairs * 2 * rows * keys,
        ),
        name="attention",
    )(q_nope, q_rope, q_mark, content, tails, w_uk, w_uv)


def shards(q_nope, q_rope, latent, doc_ids, w_uk, w_uv, w_out):
    count, heads = lax.axis_size("seq"), lax.axis_size("head")
    position = lax.axis_index("seq")
    w_rows = w_out.T
    marks = (doc_ids[:, None] == jnp.arange(MARKS, dtype=jnp.int32)[None, :]).astype(jnp.bfloat16)
    if count == 4 * PLANE and heads == 2:
        return fused(q_nope, q_rope, latent.T, doc_ids[None, :], w_uk, w_uv, w_rows)
    payload = jnp.concatenate([latent, marks], axis=1)
    q_mark = (marks - jnp.bfloat16(1)) * jnp.bfloat16(FAR)
    q_mark = jnp.concatenate([q_mark, q_mark], axis=1)
    blocks = []
    for distance in range(HOPS, 0, -1):
        block = from_behind(payload, distance)
        blocks.append(
            jnp.concatenate(
                [block[:, : LAT + ROPE], jnp.where(position >= distance, block[:, LAT + ROPE :], jnp.bfloat16(1))],
                axis=1,
            )
        )
    blocks.append(payload)
    behind = jnp.concatenate(blocks, axis=0)
    content = behind[:, :LAT]
    key_rope, key_marks = behind[:, LAT : LAT + ROPE], behind[:, LAT + ROPE :]
    tails = jnp.stack(
        [jnp.concatenate([key_rope, key_marks], axis=1), jnp.concatenate([key_marks, key_rope], axis=1)]
    )
    fixed = (q_mark, content, tails)
    attended = attention(q_nope, q_rope, *fixed, w_uk, w_uv)
    whole = lax.all_gather(w_rows, "seq", axis=0, tiled=True)
    share = product(attended, whole)
    return lax.psum_scatter(share, "head", scatter_dimension=1, tiled=True).astype(jnp.bfloat16)


def product(left, right):
    return lax.dot_general(left, right, (((1,), (1,)), ((), ())), preferred_element_type=jnp.float32)


def whole_layer(
    q_nope, q_rope, latent, doc_ids, w_uk, w_uv, w_rows, out,
    qn, qr, raw, qm, uk, uv, halo, turned, near_w, far_w, tokens, give, taken, kept, done,
    load_sem, halo_out, halo_in, near_out, near_in, far_out, far_in, pass_out, pass_in,
    token_out, token_in, share_out, share_in, result_out, result_in,
):
    rows, width = q_nope.shape
    slab = w_rows.shape[0]
    pairs = width // (2 * HD)
    slices = [(sum(SLICES[:i]), size) for i, size in enumerate(SLICES)]
    me, side = lax.axis_index("seq"), lax.axis_index("head")
    plane, row, core = me // PLANE, (me // 2) % 2, me % 2
    parity = plane % 2
    beyond = me + 4 * (1 - 2 * parity)
    mate = me + 1 - 2 * core
    across = me + 2 - 4 * row
    beyond_mate = mate + 4 * (1 - 2 * parity)
    opposite = me + 4 * (3 - 2 * plane)
    here = lambda seq: (seq, side)
    twin = (me, 1 - side)
    inner = (plane == 1) | (plane == 2)
    outer = jnp.logical_not(inner)
    keeps_near = side == plane // 2
    keeps_far = jnp.logical_not(keeps_near)

    def remote(source, target, out_sem, in_sem, device):
        return pltpu.make_async_remote_copy(
            src_ref=source, dst_ref=target, send_sem=out_sem, recv_sem=in_sem, device_id=device, device_id_type=MESH
        )

    partners = [here(beyond), here(mate), here(across), here(beyond_mate), here(opposite), twin]
    barrier = pltpu.get_barrier_semaphore()
    for partner in partners:
        pl.semaphore_signal(barrier, inc=1, device_id=partner, device_id_type=MESH)
    loads = [
        pltpu.make_async_copy(source, target, load_sem.at[i])
        for i, (source, target) in enumerate(
            [(latent, raw), (w_uk, uk), (w_uv, uv), (q_nope, qn), (q_rope, qr), (w_rows, near_w.at[row])]
        )
    ]
    loads[0].start()
    kinds = lax.broadcasted_iota(jnp.int32, (2 * MARKS, rows), 0) % MARKS
    marks = jnp.where(kinds == doc_ids[...], 1.0, 0.0).astype(jnp.float32)
    qm[...] = ((marks - 1.0) * FAR).T.astype(jnp.bfloat16)
    loads[0].wait()
    halo[HOPS * rows :] = jnp.concatenate([raw[...].astype(jnp.float32), marks[:MARKS]], axis=0).T.astype(jnp.bfloat16)
    pl.semaphore_wait(barrier, len(partners))

    def far_copy(i):
        start, size = slices[i]
        part = pl.ds(start, size)
        return remote(w_rows.at[part], far_w.at[row, part], far_out.at[i], far_in.at[i], here(opposite))

    def early_far():
        far_copy(0).start()

        @pl.when(inner)
        def _():
            for i in range(1, len(slices)):
                far_copy(i).start()


    bits = rows // (2 * BITS)

    def slot(i, part):
        start = i * rows + ((part // BITS) ^ side) * (rows // 2) + part % BITS * bits
        return halo.at[pl.ds(pl.multiple_of(start, bits), bits)]

    def step_behind(part):
        return remote(slot(HOPS, part), slot(0, part), halo_out.at[0, part], halo_in.at[0, part], here(me + PLANE))

    def step_twin(part):
        return remote(slot(0, part), slot(0, part), halo_out.at[0, BITS + part % BITS], halo_in.at[0, BITS + part % BITS], twin)

    def step_across(source, part):
        return remote(slot(source, part), slot(2, part), halo_out.at[1, part], halo_in.at[1, part], here(across))

    def step_mate(source, part):
        return remote(slot(source, part), slot(3 - 2 * core, part), halo_out.at[2, part], halo_in.at[2, part], here(mate))

    def step_second(part):
        return remote(slot(2, part), slot(1 + 2 * core, part), halo_out.at[3, part], halo_in.at[3, part], here(mate))

    def mate_wait(part):
        remote(slot(0, part), slot(1 + 2 * core, part), halo_out.at[2, part], halo_in.at[2, part], here(mate)).wait_recv()

    def second_wait(part):
        remote(slot(2, part), slot(3 - 2 * core, part), halo_out.at[3, part], halo_in.at[3, part], here(mate)).wait_recv()

    @pl.when(plane < 3)
    def _():
        for part in range(BITS):
            step_behind(part).start()

    for part in range(2 * BITS):
        pl.when(row == 0)(step_across(HOPS, part).start)
        pl.when(core == 0)(step_mate(HOPS, part).start)

    for load in loads[1:]:
        load.start()

    def pass_copy(i):
        start, size = slices[i]
        part = far_w.at[row, pl.ds(start, size)]
        return remote(part, part, pass_out.at[i], pass_in.at[i], here(across))

    def pass_wait(i):
        start, size = slices[i]
        part = far_w.at[1 - row, pl.ds(start, size)]
        remote(part, part, pass_out.at[i], pass_in.at[i], here(across)).wait_recv()

    early_far()

    @pl.when(plane == 0)
    def _():
        lanes = lax.broadcasted_iota(jnp.int32, (rows, halo.shape[1]), 1)
        halo[:rows] = jnp.where(lanes < LAT + ROPE, 0.0, 1.0).astype(jnp.bfloat16)

    for part in range(2 * BITS):
        @pl.when(plane > 0)
        def _():
            if part < BITS:
                step_behind(part).wait_recv()
                step_twin(part).start()
            else:
                step_twin(part).wait_recv()

        pl.when(row == 1)(step_across(0, part).start)
        pl.when(core == 1)(step_mate(0, part).start)
    near_copy = remote(w_rows, near_w.at[row], near_out.at[0], near_in.at[0], here(across))
    near_copy.start()
    for part in range(2 * BITS):
        step_across(0, part).wait_recv()
        step_second(part).start()
    for part in range(2 * BITS):
        mate_wait(part)
        second_wait(part)
    for load in loads[1:]:
        load.wait()
    tail = halo[:, LAT:].astype(jnp.float32)
    turned[...] = pltpu.roll(tail, ROPE, 1).astype(jnp.bfloat16)

    def columns(i):
        return pl.ds(pl.multiple_of(i * 2 * HD, 2 * HD), 2 * HD)

    def token_copy(kind, i):
        source, target, device = [(0, 1, mate), (0, 2, beyond), (2, 3, mate)][kind]
        return remote(
            tokens.at[source, :, columns(i)],
            tokens.at[target, :, columns(i)],
            token_out.at[kind, i],
            token_in.at[kind, i],
            here(device),
        )

    def relay(i):
        token_copy(1, i).wait_recv()
        token_copy(2, i).start()

    def heads(i, carry):
        tokens[0, :, columns(i)] = pair_of_heads(
            rows,
            qn[:, columns(i)],
            qr[:, pl.ds(pl.multiple_of(i * 2 * ROPE, 2 * ROPE), 2 * ROPE)],
            qm[...],
            halo[:, :LAT],
            (halo[:, LAT:], turned[...]),
            uk[:, columns(i)],
            uv[:, columns(i)],
        )
        token_copy(1, i).start()
        token_copy(0, i).start()

        @pl.when(i % 2 == 1)
        def _():
            relay(i // 2)

        return carry

    lax.fori_loop(0, pairs, heads, 0)

    def forward(i):
        far_copy(i).wait_recv()
        pass_copy(i).start()

    forward(0)

    @pl.when(inner)
    def _():
        for i in range(1, len(slices)):
            forward(i)

    def all_pairs(step):
        def body(i, carry):
            step(i)
            return carry

        return body

    def share_copy(i, blocks, part):
        where = (pl.ds(*blocks), slice(None), pl.ds(*part))
        return remote(give.at[where], taken.at[where], share_out.at[i], share_in.at[i], twin)

    def near_block(b, carry):
        share = product(near_w[...].reshape(2 * slab, width), tokens[b]).reshape(2, slab, rows)

        @pl.when(keeps_near)
        def _():
            kept[b] = share

        @pl.when(keeps_far)
        def _():
            give[b] = share.astype(jnp.bfloat16)

        return carry

    whole = (0, slab)
    near_copy_back = remote(w_rows, near_w.at[1 - row], near_out.at[0], near_in.at[0], here(across))
    near_copy_back.wait_recv()
    lax.fori_loop(0, pairs, all_pairs(lambda i: token_copy(0, i).wait_recv()), 0)
    lax.fori_loop(0, 2, near_block, 0)
    pl.when(keeps_far)(share_copy(0, (0, 2), whole).start)
    lax.fori_loop(pairs // 2, pairs - 2, all_pairs(relay), 0)

    @pl.when(outer)
    def _():
        for i in range(1, len(slices)):
            far_copy(i).start()

    lax.fori_loop(pairs - 2, pairs, all_pairs(relay), 0)
    lax.fori_loop(0, pairs, all_pairs(lambda i: token_copy(2, i).wait_recv()), 0)
    lax.fori_loop(2, 4, near_block, 0)
    pl.when(keeps_far)(share_copy(1, (2, 2), whole).start)

    def result_copy(b, unit, part, group):
        start, size = part
        target = out.at[group, :, core, pl.ds(start, size), :]
        source = done.at[b, :, pl.ds(start, size), :]
        if b == 0:
            return pltpu.make_async_copy(source, target, result_out.at[b, unit])
        device = here([mate, beyond, beyond_mate][b - 1])
        return remote(source, target, result_out.at[b, unit], result_in.at[b - 1, unit], device)

    groups = [(slices[first][0], sum(SLICES[first : last + 1]), range(first, last + 1)) for first, last in GROUPS]

    def add(i, unit, blocks, part, group):
        share_copy(i, blocks, part).wait_recv()
        first, count = blocks
        where = pl.ds(*part)
        for b in range(first, first + count):
            done[b, :, where, :] = (kept[b, :, where, :] + taken[b, :, where, :].astype(jnp.float32)).astype(jnp.bfloat16)
            if b < 2:
                result_copy(b, unit, part, group).start()

    def cross(unit, part, group):
        for b in (2, 3):
            result_copy(b, unit, part, group).start()

    def far_block(part):
        start, size = part

        def body(b, carry):
            share = product(far_w[:, pl.ds(start, size), :].reshape(2 * size, width), tokens[b]).reshape(2, size, rows)

            @pl.when(keeps_far)
            def _():
                kept[b, :, pl.ds(start, size), :] = share

            @pl.when(keeps_near)
            def _():
                give[b, :, pl.ds(start, size), :] = share.astype(jnp.bfloat16)

            return carry

        return body

    def add_far(g):
        add(2 + g, 1 + g, (0, 4), groups[g][:2], 1 - parity)

    def cross_far(g):
        cross(1 + g, groups[g][:2], 1 - parity)

    def forward_group(g):
        for i in groups[g][2]:
            forward(i)

    last = len(groups) - 1
    for g, (start, size, members) in enumerate(groups):
        if g + 1 <= last:
            @pl.when(outer)
            def _():
                forward(groups[g + 1][2][0])
                if g > 0:
                    for i in groups[g + 1][2][1:]:
                        forward(i)
        for i in members:
            pass_wait(i)
        lax.fori_loop(0, 4, far_block((start, size)), 0)
        pl.when(keeps_near)(share_copy(2 + g, (0, 4), (start, size)).start)
        if g == 0 and last > 0:
            @pl.when(outer)
            def _():
                for i in groups[1][2][1:]:
                    forward(i)
        if g == 1:
            @pl.when(keeps_near)
            def _():
                add(0, 0, (0, 2), whole, parity)
                add(1, 0, (2, 2), whole, parity)

        if g == last - 1:
            pl.when(keeps_near)(functools.partial(cross, 0, whole, parity))

            @pl.when(keeps_far)
            def _():
                for i in range(last - 1):
                    if i == last - 2:
                        add_far(i)
                    cross_far(i)
        elif 0 < g < last:
            pl.when(keeps_far)(functools.partial(add_far, g - 1))

    @pl.when(keeps_far)
    def _():
        for g in range(last - 1, last + 1):
            add_far(g)
            cross_far(g)

    def settle(units, group):
        for unit, part, blocks in units:
            for b in blocks:
                copy = result_copy(b, unit, part, group)
                if b == 0:
                    copy.wait()
                else:
                    copy.wait_send()
                    copy.wait_recv()

    @pl.when(keeps_near)
    def _():
        settle([(0, whole, range(4))], parity)
        for g, (start, size, _) in enumerate(groups):
            share_copy(2 + g, (0, 4), (start, size)).wait_send()

    @pl.when(keeps_far)
    def _():
        settle([(1 + g, (start, size), range(4)) for g, (start, size, _) in enumerate(groups)], 1 - parity)
        share_copy(0, (0, 2), whole).wait_send()
        share_copy(1, (2, 2), whole).wait_send()

    for part in range(BITS):
        pl.when(plane < 3)(step_behind(part).wait_send)
        pl.when(plane > 0)(step_twin(part).wait_send)
    for part in range(2 * BITS):
        step_across(0, part).wait_send()
        step_mate(0, part).wait_send()
        step_second(part).wait_send()
    near_copy.wait_send()
    for i in range(len(slices)):
        far_copy(i).wait_send()
        pass_copy(i).wait_send()
    for kind in range(3):
        lax.fori_loop(0, pairs, all_pairs(lambda i, kind=kind: token_copy(kind, i).wait_send()), 0)


def fused(q_nope, q_rope, latent, doc_ids, w_uk, w_uv, w_rows):
    rows, width = q_nope.shape
    slab = w_rows.shape[0]
    keys = (HOPS + 1) * rows
    pairs = width // (2 * HD)
    count, units = len(SLICES), len(GROUPS)
    assert sum(SLICES) == slab
    half = jnp.bfloat16
    copies = lambda *shape: pltpu.SemaphoreType.DMA(shape)
    result = pl.pallas_call(
        whole_layer,
        out_shape=jax.ShapeDtypeStruct((2, 2, 2, slab, rows), half),
        in_specs=[pl.BlockSpec(memory_space=pltpu.VMEM if i == 3 else pl.ANY) for i in range(7)],
        out_specs=pl.BlockSpec(memory_space=pl.ANY),
        scratch_shapes=[
            pltpu.VMEM(q_nope.shape, half),
            pltpu.VMEM(q_rope.shape, half),
            pltpu.VMEM(latent.shape, half),
            pltpu.VMEM((rows, 2 * MARKS), half),
            pltpu.VMEM(w_uk.shape, half),
            pltpu.VMEM(w_uv.shape, half),
            pltpu.VMEM((keys, latent.shape[0] + MARKS), half),
            pltpu.VMEM((keys, 2 * ROPE), half),
            pltpu.VMEM((2, slab, width), half),
            pltpu.VMEM((2, slab, width), half),
            pltpu.VMEM((4, rows, width), half),
            pltpu.VMEM((4, 2, slab, rows), half),
            pltpu.VMEM((4, 2, slab, rows), half),
            pltpu.VMEM((4, 2, slab, rows), jnp.float32),
            pltpu.VMEM((4, 2, slab, rows), half),
            copies(6), copies(4, 2 * BITS), copies(4, 2 * BITS), copies(1), copies(1), copies(count), copies(count), copies(count), copies(count),
            copies(3, pairs), copies(3, pairs), copies(2 + units), copies(2 + units), copies(4, 1 + units), copies(3, 1 + units),
        ],
        compiler_params=pltpu.CompilerParams(
            collective_id=0, has_side_effects=True, vmem_limit_bytes=56 << 20
        ),
        name="whole_layer",
    )(q_nope, q_rope, latent, doc_ids, w_uk, w_uv, w_rows)
    return result.reshape(8 * slab, rows).T


def solution(mesh):
    placed = (
        P("seq", "head"),
        P("seq", "head"),
        P("seq", None),
        P("seq"),
        P(None, "head"),
        P(None, "head"),
        P("head", "seq"),
    )
    return jax.shard_map(
        shards, mesh=mesh, in_specs=placed, out_specs=P("seq", "head"), check_vma=False
    )
```

```python
import functools
import math

import jax
import jax.numpy as jnp
from jax import lax
from jax.experimental import pallas as pl
from jax.experimental.pallas import tpu as pltpu
from jax.sharding import PartitionSpec as P

HD = 128
ROPE = 64
VD = 128
LAT = 512
HOPS = 4
MARKS = 64
FAR = 1e30
PLANE = 4
GROUPS = ((96, 1), (48, 4), (48, 4), (32, 4))
LAG = 3
BITS = 2
MESH = pl.DeviceIdType.MESH


def from_behind(value, steps):
    count = lax.axis_size("seq")
    return lax.ppermute(value, "seq", [(source, source + steps) for source in range(count - steps)])


def pair_of_heads(rows, q_nope, q_rope, q_mark, content, tails, w_uk, w_uv):
    scale = math.log2(math.e) / math.sqrt(HD + ROPE)
    keys = content.shape[0]
    key_pair = jnp.dot(content, w_uk, preferred_element_type=jnp.float32).astype(jnp.bfloat16)
    value_pair = jnp.dot(content, w_uv, preferred_element_type=jnp.float32).astype(jnp.bfloat16)
    causal = lax.broadcasted_iota(jnp.int32, (rows, rows), 1) <= lax.broadcasted_iota(jnp.int32, (rows, rows), 0)
    low = lax.broadcasted_iota(jnp.int32, (rows, 2 * ROPE), 1) < ROPE
    ones = jnp.ones((keys, VD), jnp.bfloat16)
    results = []
    for half in range(2):
        cols = slice(half * HD, (half + 1) * HD)
        rope = jnp.where(low == (half == 0), q_rope, q_mark)
        query = jnp.concatenate([q_nope[:, cols], rope], axis=1)
        key = jnp.concatenate([key_pair[:, cols], tails[half]], axis=1)
        scores = lax.dot_general(query, key, (((1,), (1,)), ((), ())), preferred_element_type=jnp.float32)
        edge = jnp.where(causal, scores[:, keys - rows :], scores[:, :rows])
        joined = jnp.concatenate([edge, scores[:, rows : keys - rows]], axis=1)
        top = jnp.max(joined, axis=-1, keepdims=True)
        raw = jnp.exp2((joined - top) * scale).astype(jnp.bfloat16)
        near = jnp.where(causal, raw[:, :rows], jnp.bfloat16(0))
        far = jnp.where(causal, jnp.bfloat16(0), raw[:, :rows])
        weights = jnp.concatenate([far, raw[:, rows:], near], axis=1)
        value = jnp.concatenate([value_pair[:, cols], ones], axis=1)
        total = jnp.dot(weights, value, preferred_element_type=jnp.float32)
        results.append((total[:, :VD] / total[:, VD:]).astype(jnp.bfloat16))
    return jnp.concatenate(results, axis=1)


def attend(rows, q_nope, q_rope, q_mark, content, tails, w_uk, w_uv, out):
    out[...] = pair_of_heads(
        rows, q_nope[...], q_rope[...], q_mark[...], content[...], (tails[0], tails[1]), w_uk[...], w_uv[...]
    )


def attention(q_nope, q_rope, q_mark, content, tails, w_uk, w_uv):
    rows, width = q_nope.shape
    keys = content.shape[0]
    pairs = width // (2 * HD)
    whole = lambda *shape: pl.BlockSpec(shape, lambda i: (0,) * len(shape))
    return pl.pallas_call(
        functools.partial(attend, rows),
        out_shape=jax.ShapeDtypeStruct((rows, width), jnp.bfloat16),
        grid=(pairs,),
        in_specs=[
            pl.BlockSpec((rows, 2 * HD), lambda i: (0, i)),
            pl.BlockSpec((rows, 2 * ROPE), lambda i: (0, i)),
            whole(rows, 2 * ROPE),
            whole(keys, LAT),
            whole(2, keys, 2 * ROPE),
            pl.BlockSpec((LAT, 2 * HD), lambda i: (0, i)),
            pl.BlockSpec((LAT, 2 * HD), lambda i: (0, i)),
        ],
        out_specs=pl.BlockSpec((rows, 2 * VD), lambda i: (0, i)),
        compiler_params=pltpu.CompilerParams(
            dimension_semantics=("arbitrary",), vmem_limit_bytes=48 << 20
        ),
        cost_estimate=pl.CostEstimate(
            flops=pairs * 2 * keys * (2 * LAT * 2 * HD + 4 * rows * 2 * HD),
            bytes_accessed=2 * (rows * width * 3 + LAT * width * 2),
            transcendentals=pairs * 2 * rows * keys,
        ),
        name="attention",
    )(q_nope, q_rope, q_mark, content, tails, w_uk, w_uv)


def shards(q_nope, q_rope, latent, doc_ids, w_uk, w_uv, w_out):
    count, heads = lax.axis_size("seq"), lax.axis_size("head")
    position = lax.axis_index("seq")
    w_rows = w_out.T
    marks = (doc_ids[:, None] == jnp.arange(MARKS, dtype=jnp.int32)[None, :]).astype(jnp.bfloat16)
    if count == 4 * PLANE and heads == 2:
        return fused(q_nope, q_rope, latent.T, doc_ids[None, :], w_uk, w_uv, w_rows)
    payload = jnp.concatenate([latent, marks], axis=1)
    q_mark = (marks - jnp.bfloat16(1)) * jnp.bfloat16(FAR)
    q_mark = jnp.concatenate([q_mark, q_mark], axis=1)
    blocks = []
    for distance in range(HOPS, 0, -1):
        block = from_behind(payload, distance)
        blocks.append(
            jnp.concatenate(
                [block[:, : LAT + ROPE], jnp.where(position >= distance, block[:, LAT + ROPE :], jnp.bfloat16(1))],
                axis=1,
            )
        )
    blocks.append(payload)
    behind = jnp.concatenate(blocks, axis=0)
    content = behind[:, :LAT]
    key_rope, key_marks = behind[:, LAT : LAT + ROPE], behind[:, LAT + ROPE :]
    tails = jnp.stack(
        [jnp.concatenate([key_rope, key_marks], axis=1), jnp.concatenate([key_marks, key_rope], axis=1)]
    )
    fixed = (q_mark, content, tails)
    attended = attention(q_nope, q_rope, *fixed, w_uk, w_uv)
    whole = lax.all_gather(w_rows, "seq", axis=0, tiled=True)
    share = product(attended, whole)
    return lax.psum_scatter(share, "head", scatter_dimension=1, tiled=True).astype(jnp.bfloat16)


def product(left, right):
    return lax.dot_general(left, right, (((1,), (1,)), ((), ())), preferred_element_type=jnp.float32)


def whole_layer(
    q_nope, q_rope, latent, doc_ids, w_uk, w_uv, w_rows, out,
    qn, qr, raw, qm, uk, uv, halo, turned, near_w, far_w, tokens, give, taken, kept, done, sums,
    load_sem, halo_out, halo_in, near_out, near_in, far_out, far_in, pass_out, pass_in,
    token_out, token_in, share_out, share_in, result_out, result_in,
):
    rows, width = q_nope.shape
    slab = w_rows.shape[0]
    pairs = width // (2 * HD)
    groups, slices = [], []
    for size, cuts in GROUPS:
        start, members = sum(group[1] for group in groups), []
        for cut in range(cuts):
            members.append(len(slices))
            slices.append((pl.ds(start, size), pl.ds(cut * width // cuts, width // cuts)))
        groups.append((start, size, members))
    me, side = lax.axis_index("seq"), lax.axis_index("head")
    plane, row, core = me // PLANE, (me // 2) % 2, me % 2
    parity = plane % 2
    beyond = me + 4 * (1 - 2 * parity)
    mate = me + 1 - 2 * core
    across = me + 2 - 4 * row
    beyond_mate = mate + 4 * (1 - 2 * parity)
    opposite = me + 4 * (3 - 2 * plane)
    here = lambda seq: (seq, side)
    twin = (me, 1 - side)
    inner = (plane == 1) | (plane == 2)
    outer = jnp.logical_not(inner)
    keeps_near = side == plane // 2
    keeps_far = jnp.logical_not(keeps_near)

    def remote(source, target, out_sem, in_sem, device):
        return pltpu.make_async_remote_copy(
            src_ref=source, dst_ref=target, send_sem=out_sem, recv_sem=in_sem, device_id=device, device_id_type=MESH
        )

    partners = [here(beyond), here(mate), here(across), here(beyond_mate), here(opposite), twin]
    barrier = pltpu.get_barrier_semaphore()
    for partner in partners:
        pl.semaphore_signal(barrier, inc=1, device_id=partner, device_id_type=MESH)
    loads = [
        pltpu.make_async_copy(source, target, load_sem.at[i])
        for i, (source, target) in enumerate(
            [(latent, raw), (w_uk, uk), (w_uv, uv), (q_nope, qn), (q_rope, qr), (w_rows, near_w.at[row])]
        )
    ]
    loads[0].start()
    kinds = lax.broadcasted_iota(jnp.int32, (2 * MARKS, rows), 0) % MARKS
    marks = jnp.where(kinds == doc_ids[...], 1.0, 0.0).astype(jnp.float32)
    qm[...] = ((marks - 1.0) * FAR).T.astype(jnp.bfloat16)
    loads[0].wait()
    halo[HOPS * rows :] = jnp.concatenate([raw[...].astype(jnp.float32), marks[:MARKS]], axis=0).T.astype(jnp.bfloat16)
    pl.semaphore_wait(barrier, len(partners))

    def far_copy(i):
        part = slices[i]
        return remote(w_rows.at[part], far_w.at[(row, *part)], far_out.at[i], far_in.at[i], here(opposite))


    bits = rows // (2 * BITS)

    def slot(i, part):
        start = i * rows + ((part // BITS) ^ side) * (rows // 2) + part % BITS * bits
        return halo.at[pl.ds(pl.multiple_of(start, bits), bits)]

    def step_behind(part):
        return remote(slot(HOPS, part), slot(0, part), halo_out.at[0, part], halo_in.at[0, part], here(me + PLANE))

    def step_twin(part):
        return remote(slot(0, part), slot(0, part), halo_out.at[0, BITS + part % BITS], halo_in.at[0, BITS + part % BITS], twin)

    def step_across(source, part):
        return remote(slot(source, part), slot(2, part), halo_out.at[1, part], halo_in.at[1, part], here(across))

    def step_mate(source, part):
        return remote(slot(source, part), slot(3 - 2 * core, part), halo_out.at[2, part], halo_in.at[2, part], here(mate))

    def step_second(part):
        return remote(slot(2, part), slot(1 + 2 * core, part), halo_out.at[3, part], halo_in.at[3, part], here(mate))

    def mate_wait(part):
        remote(slot(0, part), slot(1 + 2 * core, part), halo_out.at[2, part], halo_in.at[2, part], here(mate)).wait_recv()

    def second_wait(part):
        remote(slot(2, part), slot(3 - 2 * core, part), halo_out.at[3, part], halo_in.at[3, part], here(mate)).wait_recv()

    @pl.when(plane < 3)
    def _():
        for part in range(BITS):
            step_behind(part).start()

    for part in range(2 * BITS):
        pl.when(row == 0)(step_across(HOPS, part).start)
        pl.when(core == 0)(step_mate(HOPS, part).start)

    for load in loads[1:]:
        load.start()

    def pass_copy(i):
        part = far_w.at[(row, *slices[i])]
        return remote(part, part, pass_out.at[i], pass_in.at[i], here(across))

    def pass_wait(i):
        part = far_w.at[(1 - row, *slices[i])]
        remote(part, part, pass_out.at[i], pass_in.at[i], here(across)).wait_recv()

    pl.when(outer)(far_copy(0).start)

    @pl.when(plane == 0)
    def _():
        lanes = lax.broadcasted_iota(jnp.int32, (rows, halo.shape[1]), 1)
        halo[:rows] = jnp.where(lanes < LAT + ROPE, 0.0, 1.0).astype(jnp.bfloat16)

    for part in range(2 * BITS):
        @pl.when(plane > 0)
        def _():
            if part < BITS:
                step_behind(part).wait_recv()
                step_twin(part).start()
            else:
                step_twin(part).wait_recv()

        pl.when(row == 1)(step_across(0, part).start)
        pl.when(core == 1)(step_mate(0, part).start)
    near_copy = remote(w_rows, near_w.at[row], near_out.at[0], near_in.at[0], here(across))
    near_copy.start()
    for part in range(2 * BITS):
        step_across(0, part).wait_recv()
        step_second(part).start()
    for part in range(2 * BITS):
        mate_wait(part)
        second_wait(part)
    for load in loads[1:]:
        load.wait()
    tail = halo[:, LAT:].astype(jnp.float32)
    turned[...] = pltpu.roll(tail, ROPE, 1).astype(jnp.bfloat16)

    def columns(i):
        return pl.ds(pl.multiple_of(i * 2 * HD, 2 * HD), 2 * HD)

    def token_copy(kind, i):
        source, target, device = [(0, 1, mate), (0, 2, beyond), (2, 3, mate)][kind]
        return remote(
            tokens.at[source, :, columns(i)],
            tokens.at[target, :, columns(i)],
            token_out.at[kind, i],
            token_in.at[kind, i],
            here(device),
        )

    def relay(i):
        token_copy(1, i).wait_recv()
        token_copy(2, i).start()

    def heads(i, carry):
        tokens[0, :, columns(i)] = pair_of_heads(
            rows,
            qn[:, columns(i)],
            qr[:, pl.ds(pl.multiple_of(i * 2 * ROPE, 2 * ROPE), 2 * ROPE)],
            qm[...],
            halo[:, :LAT],
            (halo[:, LAT:], turned[...]),
            uk[:, columns(i)],
            uv[:, columns(i)],
        )
        token_copy(1, i).start()
        token_copy(0, i).start()

        @pl.when(i % 2 == 1)
        def _():
            relay(i // 2)

        return carry

    @pl.when(inner)
    def _():
        for i in range(len(slices)):
            far_copy(i).start()

    lax.fori_loop(0, pairs, heads, 0)

    def forward(i):
        far_copy(i).wait_recv()
        pass_copy(i).start()

    forward(0)

    def all_pairs(step):
        def body(i, carry):
            step(i)
            return carry

        return body

    def share_copy(i, blocks, part):
        where = (pl.ds(*blocks), slice(None), pl.ds(*part))
        return remote(give.at[where], taken.at[where], share_out.at[i], share_in.at[i], twin)

    def near_block(b, carry):
        share = product(near_w[...].reshape(2 * slab, width), tokens[b]).reshape(2, slab, rows)

        @pl.when(keeps_near)
        def _():
            kept[b] = share

        @pl.when(keeps_far)
        def _():
            give[b] = share.astype(jnp.bfloat16)

        return carry

    whole = (0, slab)
    near_copy_back = remote(w_rows, near_w.at[1 - row], near_out.at[0], near_in.at[0], here(across))
    near_copy_back.wait_recv()
    lax.fori_loop(0, pairs, all_pairs(lambda i: token_copy(0, i).wait_recv()), 0)
    lax.fori_loop(0, 2, near_block, 0)
    pl.when(keeps_far)(share_copy(0, (0, 2), whole).start)
    lax.fori_loop(pairs // 2, pairs - 2, all_pairs(relay), 0)

    @pl.when(outer)
    def _():
        for i in range(1, len(slices)):
            far_copy(i).start()

    lax.fori_loop(pairs - 2, pairs, all_pairs(relay), 0)

    @pl.when(inner)
    def _():
        for i in range(1, len(slices)):
            forward(i)

    lax.fori_loop(0, pairs, all_pairs(lambda i: token_copy(2, i).wait_recv()), 0)
    lax.fori_loop(2, 4, near_block, 0)
    pl.when(keeps_far)(share_copy(1, (2, 2), whole).start)

    def result_copy(b, unit, part, group):
        start, size = part
        target = out.at[group, :, core, pl.ds(start, size), :]
        source = done.at[b, :, pl.ds(start, size), :]
        if b == 0:
            return pltpu.make_async_copy(source, target, result_out.at[b, unit])
        device = here([mate, beyond, beyond_mate][b - 1])
        return remote(source, target, result_out.at[b, unit], result_in.at[b - 1, unit], device)

    def add(i, unit, blocks, part, group):
        share_copy(i, blocks, part).wait_recv()
        first, count = blocks
        where = pl.ds(*part)
        for b in range(first, first + count):
            done[b, :, where, :] = (kept[b, :, where, :] + taken[b, :, where, :].astype(jnp.float32)).astype(jnp.bfloat16)
            if b < 2:
                result_copy(b, unit, part, group).start()

    def cross(unit, part, group):
        for b in (2, 3):
            result_copy(b, unit, part, group).start()

    def far_block(g, i):
        start, size, members = groups[g]
        part, cut = slices[i]

        def body(b, carry):
            share = product(far_w[:, part, cut].reshape(2 * size, cut.size), tokens[b, :, cut])
            if i > members[0]:
                share += sums[b, : 2 * size]
            if i < members[-1]:
                sums[b, : 2 * size] = share
                return carry

            @pl.when(keeps_far)
            def _():
                kept[b, :, part, :] = share.reshape(2, size, rows)

            @pl.when(keeps_near)
            def _():
                give[b, :, part, :] = share.reshape(2, size, rows).astype(jnp.bfloat16)

            return carry

        return body

    def add_far(g):
        add(2 + g, 1 + g, (0, 4), groups[g][:2], 1 - parity)

    def cross_far(g):
        cross(1 + g, groups[g][:2], 1 - parity)

    last = len(groups) - 1

    def multiply(g, i):
        start, size, members = groups[g]
        pass_wait(i)
        lax.fori_loop(0, 4, far_block(g, i), 0)
        if i < members[-1]:
            return
        pl.when(keeps_near)(share_copy(2 + g, (0, 4), (start, size)).start)
        if g == 1:
            @pl.when(keeps_near)
            def _():
                add(0, 0, (0, 2), whole, parity)
                add(1, 0, (2, 2), whole, parity)

        if g == last - 1:
            pl.when(keeps_near)(functools.partial(cross, 0, whole, parity))

        @pl.when(keeps_far)
        def _():
            if 0 < g < last:
                add_far(g - 1)
            if g == last - 1:
                for earlier in range(g):
                    cross_far(earlier)

    owner = [g for g, (_, _, members) in enumerate(groups) for _ in members]
    for i in range(1, len(slices) + LAG):
        if i < len(slices):
            pl.when(outer)(functools.partial(forward, i))
        if 0 <= i - LAG:
            multiply(owner[i - LAG], i - LAG)

    @pl.when(keeps_far)
    def _():
        for g in range(last - 1, last + 1):
            add_far(g)
            cross_far(g)

    def settle(units, group):
        for unit, part, blocks in units:
            for b in blocks:
                copy = result_copy(b, unit, part, group)
                if b == 0:
                    copy.wait()
                else:
                    copy.wait_send()
                    copy.wait_recv()

    @pl.when(keeps_near)
    def _():
        settle([(0, whole, range(4))], parity)
        for g, (start, size, _) in enumerate(groups):
            share_copy(2 + g, (0, 4), (start, size)).wait_send()

    @pl.when(keeps_far)
    def _():
        settle([(1 + g, (start, size), range(4)) for g, (start, size, _) in enumerate(groups)], 1 - parity)
        share_copy(0, (0, 2), whole).wait_send()
        share_copy(1, (2, 2), whole).wait_send()

    for part in range(BITS):
        pl.when(plane < 3)(step_behind(part).wait_send)
        pl.when(plane > 0)(step_twin(part).wait_send)
    for part in range(2 * BITS):
        step_across(0, part).wait_send()
        step_mate(0, part).wait_send()
        step_second(part).wait_send()
    near_copy.wait_send()
    for i in range(len(slices)):
        far_copy(i).wait_send()
        pass_copy(i).wait_send()
    for kind in range(3):
        lax.fori_loop(0, pairs, all_pairs(lambda i, kind=kind: token_copy(kind, i).wait_send()), 0)


def fused(q_nope, q_rope, latent, doc_ids, w_uk, w_uv, w_rows):
    rows, width = q_nope.shape
    slab = w_rows.shape[0]
    keys = (HOPS + 1) * rows
    pairs = width // (2 * HD)
    count, units = sum(cuts for _, cuts in GROUPS), len(GROUPS)
    assert sum(size for size, _ in GROUPS) == slab
    half = jnp.bfloat16
    copies = lambda *shape: pltpu.SemaphoreType.DMA(shape)
    result = pl.pallas_call(
        whole_layer,
        out_shape=jax.ShapeDtypeStruct((2, 2, 2, slab, rows), half),
        in_specs=[pl.BlockSpec(memory_space=pltpu.VMEM if i == 3 else pl.ANY) for i in range(7)],
        out_specs=pl.BlockSpec(memory_space=pl.ANY),
        scratch_shapes=[
            pltpu.VMEM(q_nope.shape, half),
            pltpu.VMEM(q_rope.shape, half),
            pltpu.VMEM(latent.shape, half),
            pltpu.VMEM((rows, 2 * MARKS), half),
            pltpu.VMEM(w_uk.shape, half),
            pltpu.VMEM(w_uv.shape, half),
            pltpu.VMEM((keys, latent.shape[0] + MARKS), half),
            pltpu.VMEM((keys, 2 * ROPE), half),
            pltpu.VMEM((2, slab, width), half),
            pltpu.VMEM((2, slab, width), half),
            pltpu.VMEM((4, rows, width), half),
            pltpu.VMEM((4, 2, slab, rows), half),
            pltpu.VMEM((4, 2, slab, rows), half),
            pltpu.VMEM((4, 2, slab, rows), jnp.float32),
            pltpu.VMEM((4, 2, slab, rows), half),
            pltpu.VMEM((4, 2 * max(size for size, _ in GROUPS), rows), jnp.float32),
            copies(6), copies(4, 2 * BITS), copies(4, 2 * BITS), copies(1), copies(1), copies(count), copies(count), copies(count), copies(count),
            copies(3, pairs), copies(3, pairs), copies(2 + units), copies(2 + units), copies(4, 1 + units), copies(3, 1 + units),
        ],
        compiler_params=pltpu.CompilerParams(
            collective_id=0, has_side_effects=True, vmem_limit_bytes=56 << 20
        ),
        name="whole_layer",
    )(q_nope, q_rope, latent, doc_ids, w_uk, w_uv, w_rows)
    return result.reshape(8 * slab, rows).T


def solution(mesh):
    placed = (
        P("seq", "head"),
        P("seq", "head"),
        P("seq", None),
        P("seq"),
        P(None, "head"),
        P(None, "head"),
        P("head", "seq"),
    )
    return jax.shard_map(
        shards, mesh=mesh, in_specs=placed, out_specs=P("seq", "head"), check_vma=False
    )
```

```python
import functools
import math

import jax
import jax.numpy as jnp
from jax import lax
from jax.experimental import pallas as pl
from jax.experimental.pallas import tpu as pltpu
from jax.sharding import PartitionSpec as P

HD = 128
ROPE = 64
VD = 128
LAT = 512
HOPS = 4
MARKS = 64
FAR = 1e30
PLANE = 4
GROUPS = ((96, 1), (48, 4), (48, 4), (32, 4))
LAG = 3
BITS = 2
MESH = pl.DeviceIdType.MESH


def from_behind(value, steps):
    count = lax.axis_size("seq")
    return lax.ppermute(value, "seq", [(source, source + steps) for source in range(count - steps)])


def pair_of_heads(rows, q_nope, q_rope, q_mark, content, tails, w_uk, w_uv):
    scale = math.log2(math.e) / math.sqrt(HD + ROPE)
    keys = content.shape[0]
    key_pair = jnp.dot(content, w_uk, preferred_element_type=jnp.float32).astype(jnp.bfloat16)
    value_pair = jnp.dot(content, w_uv, preferred_element_type=jnp.float32).astype(jnp.bfloat16)
    causal = lax.broadcasted_iota(jnp.int32, (rows, rows), 1) <= lax.broadcasted_iota(jnp.int32, (rows, rows), 0)
    low = lax.broadcasted_iota(jnp.int32, (rows, 2 * ROPE), 1) < ROPE
    ones = jnp.ones((keys, VD), jnp.bfloat16)
    results = []
    for half in range(2):
        cols = slice(half * HD, (half + 1) * HD)
        rope = jnp.where(low == (half == 0), q_rope, q_mark)
        query = jnp.concatenate([q_nope[:, cols], rope], axis=1)
        key = jnp.concatenate([key_pair[:, cols], tails[half]], axis=1)
        scores = lax.dot_general(query, key, (((1,), (1,)), ((), ())), preferred_element_type=jnp.float32)
        edge = jnp.where(causal, scores[:, keys - rows :], scores[:, :rows])
        joined = jnp.concatenate([edge, scores[:, rows : keys - rows]], axis=1)
        top = jnp.max(joined, axis=-1, keepdims=True)
        raw = jnp.exp2((joined - top) * scale).astype(jnp.bfloat16)
        near = jnp.where(causal, raw[:, :rows], jnp.bfloat16(0))
        far = jnp.where(causal, jnp.bfloat16(0), raw[:, :rows])
        weights = jnp.concatenate([far, raw[:, rows:], near], axis=1)
        value = jnp.concatenate([value_pair[:, cols], ones], axis=1)
        total = jnp.dot(weights, value, preferred_element_type=jnp.float32)
        results.append((total[:, :VD] / total[:, VD:]).astype(jnp.bfloat16))
    return jnp.concatenate(results, axis=1)


def attend(rows, q_nope, q_rope, q_mark, content, tails, w_uk, w_uv, out):
    out[...] = pair_of_heads(
        rows, q_nope[...], q_rope[...], q_mark[...], content[...], (tails[0], tails[1]), w_uk[...], w_uv[...]
    )


def attention(q_nope, q_rope, q_mark, content, tails, w_uk, w_uv):
    rows, width = q_nope.shape
    keys = content.shape[0]
    pairs = width // (2 * HD)
    whole = lambda *shape: pl.BlockSpec(shape, lambda i: (0,) * len(shape))
    return pl.pallas_call(
        functools.partial(attend, rows),
        out_shape=jax.ShapeDtypeStruct((rows, width), jnp.bfloat16),
        grid=(pairs,),
        in_specs=[
            pl.BlockSpec((rows, 2 * HD), lambda i: (0, i)),
            pl.BlockSpec((rows, 2 * ROPE), lambda i: (0, i)),
            whole(rows, 2 * ROPE),
            whole(keys, LAT),
            whole(2, keys, 2 * ROPE),
            pl.BlockSpec((LAT, 2 * HD), lambda i: (0, i)),
            pl.BlockSpec((LAT, 2 * HD), lambda i: (0, i)),
        ],
        out_specs=pl.BlockSpec((rows, 2 * VD), lambda i: (0, i)),
        compiler_params=pltpu.CompilerParams(
            dimension_semantics=("arbitrary",), vmem_limit_bytes=48 << 20
        ),
        cost_estimate=pl.CostEstimate(
            flops=pairs * 2 * keys * (2 * LAT * 2 * HD + 4 * rows * 2 * HD),
            bytes_accessed=2 * (rows * width * 3 + LAT * width * 2),
            transcendentals=pairs * 2 * rows * keys,
        ),
        name="attention",
    )(q_nope, q_rope, q_mark, content, tails, w_uk, w_uv)


def shards(q_nope, q_rope, latent, doc_ids, w_uk, w_uv, w_out):
    count, heads = lax.axis_size("seq"), lax.axis_size("head")
    position = lax.axis_index("seq")
    w_rows = w_out.T
    marks = (doc_ids[:, None] == jnp.arange(MARKS, dtype=jnp.int32)[None, :]).astype(jnp.bfloat16)
    if count == 4 * PLANE and heads == 2:
        return fused(q_nope, q_rope, latent.T, doc_ids[None, :], w_uk, w_uv, w_rows)
    payload = jnp.concatenate([latent, marks], axis=1)
    q_mark = (marks - jnp.bfloat16(1)) * jnp.bfloat16(FAR)
    q_mark = jnp.concatenate([q_mark, q_mark], axis=1)
    blocks = []
    for distance in range(HOPS, 0, -1):
        block = from_behind(payload, distance)
        blocks.append(
            jnp.concatenate(
                [block[:, : LAT + ROPE], jnp.where(position >= distance, block[:, LAT + ROPE :], jnp.bfloat16(1))],
                axis=1,
            )
        )
    blocks.append(payload)
    behind = jnp.concatenate(blocks, axis=0)
    content = behind[:, :LAT]
    key_rope, key_marks = behind[:, LAT : LAT + ROPE], behind[:, LAT + ROPE :]
    tails = jnp.stack(
        [jnp.concatenate([key_rope, key_marks], axis=1), jnp.concatenate([key_marks, key_rope], axis=1)]
    )
    fixed = (q_mark, content, tails)
    attended = attention(q_nope, q_rope, *fixed, w_uk, w_uv)
    whole = lax.all_gather(w_rows, "seq", axis=0, tiled=True)
    share = product(attended, whole)
    return lax.psum_scatter(share, "head", scatter_dimension=1, tiled=True).astype(jnp.bfloat16)


def product(left, right):
    return lax.dot_general(left, right, (((1,), (1,)), ((), ())), preferred_element_type=jnp.float32)


def whole_layer(
    q_nope, q_rope, latent, doc_ids, w_uk, w_uv, w_rows, out,
    qn, qr, raw, qm, uk, uv, halo, turned, near_w, far_w, tokens, give, taken, kept, done, sums,
    load_sem, halo_out, halo_in, near_out, near_in, far_out, far_in, pass_out, pass_in,
    token_out, token_in, share_out, share_in, result_out, result_in,
):
    rows, width = q_nope.shape
    slab = w_rows.shape[0]
    pairs = width // (2 * HD)
    groups, slices = [], []
    for size, cuts in GROUPS:
        start, members = sum(group[1] for group in groups), []
        for cut in range(cuts):
            members.append(len(slices))
            slices.append((pl.ds(start, size), pl.ds(cut * width // cuts, width // cuts)))
        groups.append((start, size, members))
    me, side = lax.axis_index("seq"), lax.axis_index("head")
    plane, row, core = me // PLANE, (me // 2) % 2, me % 2
    parity = plane % 2
    beyond = me + 4 * (1 - 2 * parity)
    mate = me + 1 - 2 * core
    across = me + 2 - 4 * row
    beyond_mate = mate + 4 * (1 - 2 * parity)
    opposite = me + 4 * (3 - 2 * plane)
    here = lambda seq: (seq, side)
    twin = (me, 1 - side)
    inner = (plane == 1) | (plane == 2)
    outer = jnp.logical_not(inner)
    keeps_near = side == plane // 2
    keeps_far = jnp.logical_not(keeps_near)

    def remote(source, target, out_sem, in_sem, device):
        return pltpu.make_async_remote_copy(
            src_ref=source, dst_ref=target, send_sem=out_sem, recv_sem=in_sem, device_id=device, device_id_type=MESH
        )

    partners = [here(beyond), here(mate), here(across), here(beyond_mate), here(opposite), twin]
    barrier = pltpu.get_barrier_semaphore()
    for partner in partners:
        pl.semaphore_signal(barrier, inc=1, device_id=partner, device_id_type=MESH)
    loads = [
        pltpu.make_async_copy(source, target, load_sem.at[i])
        for i, (source, target) in enumerate(
            [(latent, raw), (w_uk, uk), (w_uv, uv), (q_nope, qn), (q_rope, qr), (w_rows, near_w.at[row])]
        )
    ]
    loads[0].start()
    kinds = lax.broadcasted_iota(jnp.int32, (2 * MARKS, rows), 0) % MARKS
    marks = jnp.where(kinds == doc_ids[...], 1.0, 0.0).astype(jnp.float32)
    qm[...] = ((marks - 1.0) * FAR).T.astype(jnp.bfloat16)
    loads[0].wait()
    halo[HOPS * rows :] = jnp.concatenate([raw[...].astype(jnp.float32), marks[:MARKS]], axis=0).T.astype(jnp.bfloat16)
    pl.semaphore_wait(barrier, len(partners))

    def far_copy(i):
        part = slices[i]
        return remote(w_rows.at[part], far_w.at[(row, *part)], far_out.at[i], far_in.at[i], here(opposite))


    bits = rows // (2 * BITS)

    def slot(i, part):
        start = i * rows + ((part // BITS) ^ side) * (rows // 2) + part % BITS * bits
        return halo.at[pl.ds(pl.multiple_of(start, bits), bits)]

    def step_behind(part):
        return remote(slot(HOPS, part), slot(0, part), halo_out.at[0, part], halo_in.at[0, part], here(me + PLANE))

    def step_twin(part):
        return remote(slot(0, part), slot(0, part), halo_out.at[0, BITS + part % BITS], halo_in.at[0, BITS + part % BITS], twin)

    def step_across(source, part):
        return remote(slot(source, part), slot(2, part), halo_out.at[1, part], halo_in.at[1, part], here(across))

    def step_mate(source, part):
        return remote(slot(source, part), slot(3 - 2 * core, part), halo_out.at[2, part], halo_in.at[2, part], here(mate))

    def step_second(part):
        return remote(slot(2, part), slot(1 + 2 * core, part), halo_out.at[3, part], halo_in.at[3, part], here(mate))

    def mate_wait(part):
        remote(slot(0, part), slot(1 + 2 * core, part), halo_out.at[2, part], halo_in.at[2, part], here(mate)).wait_recv()

    def second_wait(part):
        remote(slot(2, part), slot(3 - 2 * core, part), halo_out.at[3, part], halo_in.at[3, part], here(mate)).wait_recv()

    @pl.when(plane < 3)
    def _():
        for part in range(BITS):
            step_behind(part).start()

    for part in range(2 * BITS):
        pl.when(row == 0)(step_across(HOPS, part).start)
        pl.when(core == 0)(step_mate(HOPS, part).start)

    for load in loads[1:]:
        load.start()

    def pass_copy(i):
        part = far_w.at[(row, *slices[i])]
        return remote(part, part, pass_out.at[i], pass_in.at[i], here(across))

    def pass_wait(i):
        part = far_w.at[(1 - row, *slices[i])]
        remote(part, part, pass_out.at[i], pass_in.at[i], here(across)).wait_recv()

    pl.when(outer)(far_copy(0).start)

    @pl.when(plane == 0)
    def _():
        lanes = lax.broadcasted_iota(jnp.int32, (rows, halo.shape[1]), 1)
        halo[:rows] = jnp.where(lanes < LAT + ROPE, 0.0, 1.0).astype(jnp.bfloat16)

    for part in range(2 * BITS):
        @pl.when(plane > 0)
        def _():
            if part < BITS:
                step_behind(part).wait_recv()
                step_twin(part).start()
            else:
                step_twin(part).wait_recv()

        pl.when(row == 1)(step_across(0, part).start)
        pl.when(core == 1)(step_mate(0, part).start)
    near_copy = remote(w_rows, near_w.at[row], near_out.at[0], near_in.at[0], here(across))
    near_copy.start()
    for part in range(2 * BITS):
        step_across(0, part).wait_recv()
        step_second(part).start()
    for part in range(2 * BITS):
        mate_wait(part)
        second_wait(part)
    for load in loads[1:]:
        load.wait()
    tail = halo[:, LAT:].astype(jnp.float32)
    turned[...] = pltpu.roll(tail, ROPE, 1).astype(jnp.bfloat16)

    def columns(i):
        return pl.ds(pl.multiple_of(i * 2 * HD, 2 * HD), 2 * HD)

    def token_copy(kind, i):
        source, target, device = [(0, 1, mate), (0, 2, beyond), (2, 3, mate)][kind]
        return remote(
            tokens.at[source, :, columns(i)],
            tokens.at[target, :, columns(i)],
            token_out.at[kind, i],
            token_in.at[kind, i],
            here(device),
        )

    def relay(i):
        token_copy(1, i).wait_recv()
        token_copy(2, i).start()

    def heads(i, carry):
        tokens[0, :, columns(i)] = pair_of_heads(
            rows,
            qn[:, columns(i)],
            qr[:, pl.ds(pl.multiple_of(i * 2 * ROPE, 2 * ROPE), 2 * ROPE)],
            qm[...],
            halo[:, :LAT],
            (halo[:, LAT:], turned[...]),
            uk[:, columns(i)],
            uv[:, columns(i)],
        )
        token_copy(1, i).start()
        token_copy(0, i).start()

        @pl.when(i % 2 == 1)
        def _():
            relay(i // 2)

        return carry

    @pl.when(inner)
    def _():
        for i in range(len(slices)):
            far_copy(i).start()

    lax.fori_loop(0, pairs, heads, 0)

    def forward(i):
        far_copy(i).wait_recv()
        pass_copy(i).start()

    forward(0)

    def all_pairs(step):
        def body(i, carry):
            step(i)
            return carry

        return body

    def share_copy(i, blocks, part):
        where = (pl.ds(*blocks), slice(None), pl.ds(*part))
        return remote(give.at[where], taken.at[where], share_out.at[i], share_in.at[i], twin)

    def near_block(b, carry):
        share = product(near_w[...].reshape(2 * slab, width), tokens[b]).reshape(2, slab, rows)

        @pl.when(keeps_near)
        def _():
            kept[b] = share

        @pl.when(keeps_far)
        def _():
            give[b] = share.astype(jnp.bfloat16)

        return carry

    whole = (0, slab)
    near_copy_back = remote(w_rows, near_w.at[1 - row], near_out.at[0], near_in.at[0], here(across))
    near_copy_back.wait_recv()
    lax.fori_loop(0, pairs, all_pairs(lambda i: token_copy(0, i).wait_recv()), 0)
    lax.fori_loop(0, 2, near_block, 0)
    pl.when(keeps_far)(share_copy(0, (0, 2), whole).start)
    lax.fori_loop(pairs // 2, pairs - 2, all_pairs(relay), 0)

    @pl.when(outer)
    def _():
        for i in range(1, len(slices)):
            far_copy(i).start()

    lax.fori_loop(pairs - 2, pairs, all_pairs(relay), 0)

    @pl.when(inner)
    def _():
        for i in range(1, len(slices)):
            forward(i)

    lax.fori_loop(0, pairs, all_pairs(lambda i: token_copy(2, i).wait_recv()), 0)
    lax.fori_loop(2, 4, near_block, 0)
    pl.when(keeps_far)(share_copy(1, (2, 2), whole).start)

    def result_copy(b, unit, part, group):
        start, size = part
        target = out.at[group, :, core, pl.ds(start, size), :]
        source = done.at[b, :, pl.ds(start, size), :]
        if b == 0:
            return pltpu.make_async_copy(source, target, result_out.at[b, unit])
        device = here([mate, beyond, beyond_mate][b - 1])
        return remote(source, target, result_out.at[b, unit], result_in.at[b - 1, unit], device)

    def add(i, unit, blocks, part, group, held=2):
        share_copy(i, blocks, part).wait_recv()
        first, count = blocks
        where = pl.ds(*part)
        for b in range(first, first + count):
            done[b, :, where, :] = (kept[b, :, where, :] + taken[b, :, where, :].astype(jnp.float32)).astype(jnp.bfloat16)
            if b < held:
                result_copy(b, unit, part, group).start()

    def cross(unit, part, group):
        for b in (2, 3):
            result_copy(b, unit, part, group).start()

    def far_block(g, i):
        start, size, members = groups[g]
        part, cut = slices[i]

        def body(b, carry):
            share = product(far_w[:, part, cut].reshape(2 * size, cut.size), tokens[b, :, cut])
            if i > members[0]:
                share += sums[b, : 2 * size]
            if i < members[-1]:
                sums[b, : 2 * size] = share
                return carry

            @pl.when(keeps_far)
            def _():
                kept[b, :, part, :] = share.reshape(2, size, rows)

            @pl.when(keeps_near)
            def _():
                give[b, :, part, :] = share.reshape(2, size, rows).astype(jnp.bfloat16)

            return carry

        return body

    def add_far(g):
        for i, first in enumerate((2, 0)):
            add(2 + 2 * g + i, 1 + g, (first, 2), groups[g][:2], 1 - parity, 4)

    last = len(groups) - 1

    def multiply(g, i):
        start, size, members = groups[g]
        pass_wait(i)
        for at, first in enumerate((2, 0)):
            lax.fori_loop(first, first + 2, far_block(g, i), 0)
            if i == members[-1]:
                pl.when(keeps_near)(share_copy(2 + 2 * g + at, (first, 2), (start, size)).start)
        if i < members[-1]:
            return
        if g == 1:
            @pl.when(keeps_near)
            def _():
                add(0, 0, (0, 2), whole, parity)
                add(1, 0, (2, 2), whole, parity)

        if g == last - 1:
            pl.when(keeps_near)(functools.partial(cross, 0, whole, parity))

        @pl.when(keeps_far)
        def _():
            if 0 < g < last:
                add_far(g - 1)

    owner = [g for g, (_, _, members) in enumerate(groups) for _ in members]
    for i in range(1, len(slices) + LAG):
        if i < len(slices):
            pl.when(outer)(functools.partial(forward, i))
        if 0 <= i - LAG:
            multiply(owner[i - LAG], i - LAG)

    @pl.when(keeps_far)
    def _():
        for g in range(last - 1, last + 1):
            add_far(g)

    def settle(units, group):
        for unit, part, blocks in units:
            for b in blocks:
                copy = result_copy(b, unit, part, group)
                if b == 0:
                    copy.wait()
                else:
                    copy.wait_send()
                    copy.wait_recv()

    @pl.when(keeps_near)
    def _():
        settle([(0, whole, range(4))], parity)
        for g, (start, size, _) in enumerate(groups):
            for at, first in enumerate((2, 0)):
                share_copy(2 + 2 * g + at, (first, 2), (start, size)).wait_send()

    @pl.when(keeps_far)
    def _():
        settle([(1 + g, (start, size), range(4)) for g, (start, size, _) in enumerate(groups)], 1 - parity)
        share_copy(0, (0, 2), whole).wait_send()
        share_copy(1, (2, 2), whole).wait_send()

    for part in range(BITS):
        pl.when(plane < 3)(step_behind(part).wait_send)
        pl.when(plane > 0)(step_twin(part).wait_send)
    for part in range(2 * BITS):
        step_across(0, part).wait_send()
        step_mate(0, part).wait_send()
        step_second(part).wait_send()
    near_copy.wait_send()
    for i in range(len(slices)):
        far_copy(i).wait_send()
        pass_copy(i).wait_send()
    for kind in range(3):
        lax.fori_loop(0, pairs, all_pairs(lambda i, kind=kind: token_copy(kind, i).wait_send()), 0)


def fused(q_nope, q_rope, latent, doc_ids, w_uk, w_uv, w_rows):
    rows, width = q_nope.shape
    slab = w_rows.shape[0]
    keys = (HOPS + 1) * rows
    pairs = width // (2 * HD)
    count, units = sum(cuts for _, cuts in GROUPS), len(GROUPS)
    assert sum(size for size, _ in GROUPS) == slab
    half = jnp.bfloat16
    copies = lambda *shape: pltpu.SemaphoreType.DMA(shape)
    result = pl.pallas_call(
        whole_layer,
        out_shape=jax.ShapeDtypeStruct((2, 2, 2, slab, rows), half),
        in_specs=[pl.BlockSpec(memory_space=pltpu.VMEM if i == 3 else pl.ANY) for i in range(7)],
        out_specs=pl.BlockSpec(memory_space=pl.ANY),
        scratch_shapes=[
            pltpu.VMEM(q_nope.shape, half),
            pltpu.VMEM(q_rope.shape, half),
            pltpu.VMEM(latent.shape, half),
            pltpu.VMEM((rows, 2 * MARKS), half),
            pltpu.VMEM(w_uk.shape, half),
            pltpu.VMEM(w_uv.shape, half),
            pltpu.VMEM((keys, latent.shape[0] + MARKS), half),
            pltpu.VMEM((keys, 2 * ROPE), half),
            pltpu.VMEM((2, slab, width), half),
            pltpu.VMEM((2, slab, width), half),
            pltpu.VMEM((4, rows, width), half),
            pltpu.VMEM((4, 2, slab, rows), half),
            pltpu.VMEM((4, 2, slab, rows), half),
            pltpu.VMEM((4, 2, slab, rows), jnp.float32),
            pltpu.VMEM((4, 2, slab, rows), half),
            pltpu.VMEM((4, 2 * max(size for size, _ in GROUPS), rows), jnp.float32),
            copies(6), copies(4, 2 * BITS), copies(4, 2 * BITS), copies(1), copies(1), copies(count), copies(count), copies(count), copies(count),
            copies(3, pairs), copies(3, pairs), copies(2 + 2 * units), copies(2 + 2 * units), copies(4, 1 + units), copies(3, 1 + units),
        ],
        compiler_params=pltpu.CompilerParams(
            collective_id=0, has_side_effects=True, vmem_limit_bytes=56 << 20
        ),
        name="whole_layer",
    )(q_nope, q_rope, latent, doc_ids, w_uk, w_uv, w_rows)
    return result.reshape(8 * slab, rows).T


def solution(mesh):
    placed = (
        P("seq", "head"),
        P("seq", "head"),
        P("seq", None),
        P("seq"),
        P(None, "head"),
        P(None, "head"),
        P("head", "seq"),
    )
    return jax.shard_map(
        shards, mesh=mesh, in_specs=placed, out_specs=P("seq", "head"), check_vma=False
    )
```
